512 devices in a mesh: section: 4 (over x), ctx: 64 (over z, y), tp: 2 (over core).
Axes of the slice: x: 4, y: 8, z: 8, core: 2. Of those that a mesh axis runs over, the one named last changes fastest.
Arguments:
- section_input: float32 [4, 8192, 4096], P('section', 'ctx', 'tp'), may hold values from -60 to 60
- long_filter: bfloat16 [4, 8192, 256], P('section', 'ctx', 'tp'), may hold values from -2 to 2
- short_filter: bfloat16 [4, 3, 3, 4096], P('section', None, None, 'tp'), may hold values from -12 to 12
- skip_gain: float32 [4, 4096], P('section', 'tp'), may hold values from -1 to 1
Outputs:
- received: float32 [4, 8192, 4096], P('section', 'ctx', 'tp')
The draws below stay inside these ranges and needn't reach their ends.
All inputs are finite; a program needn't handle non-finite values.
Results may differ from the reference program's by a relative error of at most 0.009.
Values may be sent and summed in bfloat16 or wider, within the bound.
A program may use at most 64 MiB of HBM per device.

```python
import math
import jax
import jax.numpy as jnp
from jax import lax

CHAN = 4096
GROUP = 16
TAPS = 3
BLOCK = 128
SEQ = 8192
FILTERS = 256
N_SECTION = 4


def channel_scale(key, spread):
    ranks = jax.random.permutation(jax.random.fold_in(key, 11), CHAN).astype(jnp.float32)
    return jnp.exp(math.log(spread) * ((ranks + 0.5) / CHAN - 0.5))


def draw_section_input(key, part):
    key_entries, key_rows = jax.random.split(key)
    column_scale = channel_scale(key, 10.0)[None, None, :]
    row_scale = jnp.exp(jax.random.uniform(key_rows, (N_SECTION, SEQ, 1), jnp.float32, math.log(0.3), math.log(3.0)))
    entries = jax.random.truncated_normal(key_entries, -6.0, 6.0, (N_SECTION, SEQ, CHAN), jnp.float32)
    return entries * row_scale * column_scale


def draw_short_filter(key, part):
    key_entries = jax.random.fold_in(key, 23)
    column_scale = channel_scale(key, 10.0)
    entries = jax.random.truncated_normal(key_entries, -3.0, 3.0, (N_SECTION, 3, TAPS, CHAN), jnp.float32)
    return (entries / column_scale[None, None, None, :]).astype(jnp.bfloat16)


def draw_long_filter(key, part):
    key_rates, key_entries = jax.random.split(key)
    lags = jnp.arange(SEQ, dtype=jnp.float32)[None, :, None]
    log_span = jax.random.uniform(key_rates, (N_SECTION, 1, FILTERS), jnp.float32, math.log(30.0), math.log(256.0 * SEQ))
    entries = jax.random.truncated_normal(key_entries, -6.0, 6.0, (N_SECTION, SEQ, FILTERS), jnp.float32)
    decay_rate = jnp.exp(-log_span)
    energy = jnp.expm1(-2.0 * decay_rate) / jnp.expm1(-2.0 * decay_rate * SEQ)
    return (entries * jnp.exp(-decay_rate * lags) * jnp.sqrt(energy)).astype(jnp.bfloat16)


def levels(rng, dims, cuts, least, high):
    factor_of = 1.0
    for dim, parts in cuts:
        heights = jax.random.uniform(jax.random.fold_in(jax.random.fold_in(rng, 6), dim), (parts,), jnp.float32, least / len(cuts), high / len(cuts))
        factor_of = factor_of * jnp.repeat(jnp.exp(heights), dims[dim] // parts).reshape((-1,) + (1,) * (len(dims) - 1 - dim))
    return factor_of


def setup_inputs(seed: int = 0) -> dict:
    keys = jax.random.split(jax.random.key(seed), 5)
    section_input = draw_section_input(jax.random.fold_in(keys[4], 71), 0)
    long_filter = draw_long_filter(jax.random.fold_in(keys[4], 71), 0)
    short_filter = draw_short_filter(jax.random.fold_in(keys[4], 71), 0)
    skip_gain = jnp.clip(jax.random.uniform(keys[3], (N_SECTION, CHAN), jnp.float32, -1.0, 1.0) * levels(keys[3], (N_SECTION, CHAN), ((0, 4), (1, 2)), -0.4, 0.0), -1.0, 1.0)
    return dict(section_input=section_input, long_filter=long_filter, short_filter=short_filter, skip_gain=skip_gain)


TWO_PI = 6.283185307179586

def unit_pair(position, period):
    mirror = period - position
    folded = jnp.minimum(position, mirror)
    angle_value = folded.astype(jnp.float32) * (TWO_PI / period)
    cosine = jnp.where(4 * folded == period, 0.0, jnp.cos(angle_value)).astype(jnp.float32)
    sine_part = jnp.where((folded == 0) | (2 * folded == period), 0.0, jnp.sin(angle_value)).astype(jnp.float32)
    sine_part = jnp.where(position > mirror, -sine_part, sine_part)
    return (cosine, -sine_part)

def first_section(table_re, table_im, data):
    plain = data.astype(jnp.float32)
    real_out = jnp.einsum('ka,abc->kbc', table_re.astype(jnp.float32), plain)
    imag_out = jnp.einsum('ka,abc->kbc', table_im.astype(jnp.float32), plain)
    return (real_out.astype(jnp.bfloat16), imag_out.astype(jnp.bfloat16))

def rotate(turn_re, turn_im, data_re, data_im):
    plain_re = data_re.astype(jnp.float32)
    plain_im = data_im.astype(jnp.float32)
    real_out = turn_re[:, :, None] * plain_re - turn_im[:, :, None] * plain_im
    imag_out = turn_re[:, :, None] * plain_im + turn_im[:, :, None] * plain_re
    return (real_out.astype(jnp.bfloat16), imag_out.astype(jnp.bfloat16))

def mix_rows(form, table_re, table_im, data_re, data_im):

    def product_of(left, right):
        return jnp.einsum(form, left.astype(jnp.float32), right.astype(jnp.float32))
    real_out = product_of(table_re, data_re) - product_of(table_im, data_im)
    imag_out = product_of(table_re, data_im) + product_of(table_im, data_re)
    return (real_out, imag_out)

def apply_filter(spec_re, spec_im, filt_re, filt_im):
    rows_count, inner_width, channels = spec_re.shape
    filters = filt_re.shape[2]
    grouped_shape = (rows_count, inner_width, filters, channels // filters)
    grouped_re = spec_re.reshape(grouped_shape)
    grouped_im = spec_im.reshape(grouped_shape)
    gain_re = filt_re[..., None]
    gain_im = filt_im[..., None]
    out_re = (grouped_re * gain_re - grouped_im * gain_im).reshape(spec_re.shape)
    out_im = (grouped_re * gain_im + grouped_im * gain_re).reshape(spec_re.shape)
    return (out_re.astype(jnp.bfloat16), out_im.astype(jnp.bfloat16))

def convolve(product, kernel):
    half_span = SEQ // BLOCK
    full_span = 2 * half_span
    freq_total = full_span * BLOCK
    block_ids = jnp.arange(half_span, dtype=jnp.int32)
    freq_rows = jnp.arange(full_span, dtype=jnp.int32)
    inner_ids = jnp.arange(BLOCK, dtype=jnp.int32)
    outer_re, outer_im = unit_pair(freq_rows[:, None] * block_ids[None, :] % full_span, full_span)
    outer_re = outer_re.astype(jnp.bfloat16)
    outer_im = outer_im.astype(jnp.bfloat16)
    inner_re, inner_im = unit_pair(inner_ids[:, None] * inner_ids[None, :] % BLOCK, BLOCK)
    inner_re = inner_re.astype(jnp.bfloat16)
    inner_im = inner_im.astype(jnp.bfloat16)
    turn_re, turn_im = unit_pair(freq_rows[:, None] * inner_ids[None, :] % freq_total, freq_total)
    kernel_blocks = kernel.reshape(half_span, BLOCK, FILTERS)
    kern_re, kern_im = first_section(outer_re, outer_im, kernel_blocks)
    kern_re, kern_im = rotate(turn_re, turn_im, kern_re, kern_im)
    filt_re, filt_im = mix_rows('qb,rbc->rqc', inner_re, inner_im, kern_re, kern_im)
    block_width = math.gcd(CHAN, 256)
    block_count = CHAN // block_width
    signal_blocks = product.reshape(half_span, BLOCK, block_count, block_width).transpose(2, 0, 1, 3)
    filt_re_blocks = filt_re.reshape(full_span, BLOCK, block_count, block_width // GROUP).transpose(2, 0, 1, 3)
    filt_im_blocks = filt_im.reshape(full_span, BLOCK, block_count, block_width // GROUP).transpose(2, 0, 1, 3)

    def one_block(pieces):
        signal_part, filt_re_part, filt_im_part = pieces
        first_re, first_im = first_section(outer_re, outer_im, signal_part)
        turned_re, turned_im = rotate(turn_re, turn_im, first_re, first_im)
        spec_re, spec_im = mix_rows('qb,rbc->rqc', inner_re, inner_im, turned_re, turned_im)
        weight_re, weight_im = apply_filter(spec_re, spec_im, filt_re_part, filt_im_part)
        back_re, back_im = mix_rows('bq,rqc->rbc', inner_re, -inner_im, weight_re, weight_im)
        unturn_re, unturn_im = rotate(turn_re, -turn_im, back_re, back_im)
        conv_part = jnp.einsum('ka,kbc->abc', outer_re.astype(jnp.float32), unturn_re.astype(jnp.float32))
        conv_part = conv_part + jnp.einsum('ka,kbc->abc', outer_im.astype(jnp.float32), unturn_im.astype(jnp.float32))
        return (conv_part * (1.0 / freq_total)).astype(jnp.bfloat16)
    results = lax.map(one_block, (signal_blocks, filt_re_blocks, filt_im_blocks))
    return results.transpose(1, 2, 0, 3).reshape(SEQ, CHAN)

def layer(acts, kernel, short_taps, skip_row):
    squares = lax.optimization_barrier(jnp.sum(acts * acts, axis=1, keepdims=True)) / CHAN
    normed = (acts * lax.rsqrt(squares + 1e-06)).astype(jnp.bfloat16)
    padded = jnp.concatenate([jnp.zeros((TAPS - 1, CHAN), jnp.bfloat16), normed], axis=0).astype(jnp.float32)
    taps_all = short_taps.astype(jnp.float32)
    featured = []
    for feature_id in range(3):
        running = jnp.zeros((SEQ, CHAN), jnp.float32)
        for offset in range(TAPS):
            begin_row = TAPS - 1 - offset
            running = running + taps_all[feature_id, offset][None, :] * padded[begin_row:begin_row + SEQ]
        featured.append(running)
    query = featured[0].astype(jnp.bfloat16)
    product = (featured[1] * featured[2]).astype(jnp.bfloat16)
    conv = convolve(product, kernel)
    return acts + query.astype(jnp.float32) * (conv.astype(jnp.float32) + skip_row[None, :] * product.astype(jnp.float32))

def reference(section_input, long_filter, short_filter, skip_gain):
    finished = []
    for section_id in range(N_SECTION):
        finished.append(layer(section_input[section_id], long_filter[section_id], short_filter[section_id], skip_gain[section_id]))
    return jnp.roll(jnp.stack(finished), 1, axis=0)
```

```python
import jax
import jax.numpy as jnp
import numpy as np
from jax import lax
from jax.sharding import PartitionSpec as P

CHAN = 4096
GROUP = 16
TAPS = 3
BLOCK = 128
SEQ = 8192
HALF = SEQ // BLOCK
SPAN = 2 * HALF
TOTAL = SPAN * BLOCK
ROWS = HALF + 1


def unit_pair(position, period):
    mirror = period - position
    folded = np.minimum(position, mirror)
    angle = folded.astype(np.float32) * np.float32(2 * np.pi / period)
    cosine = np.where(4 * folded == period, 0.0, np.cos(angle)).astype(np.float32)
    sine = np.where((folded == 0) | (2 * folded == period), 0.0, np.sin(angle)).astype(np.float32)
    sine = np.where(position > mirror, -sine, sine)
    return cosine, -sine


def tables():
    k1 = np.arange(ROWS)
    a = np.arange(HALF)
    b = np.arange(BLOCK)
    outer = unit_pair(k1[:, None] * a[None, :] % SPAN, SPAN)
    inner = unit_pair(b[:, None] * b[None, :] % BLOCK, BLOCK)
    turn = unit_pair(k1[:, None] * b[None, :] % TOTAL, TOTAL)
    return outer, inner, turn


def from_behind(block, axis, distance):
    devices = range(lax.axis_size(axis))
    route = [(i - distance, i) for i in devices if i - distance in devices]
    return lax.ppermute(block, axis, route)


def passed_along(x, axis, by):
    peers = lax.axis_size(axis)
    return lax.ppermute(x, axis, [(i, (i + by) % peers) for i in range(peers)])


def rotate(turn_re, turn_im, re, im):
    return (
        (turn_re * re - turn_im * im).astype(jnp.bfloat16),
        (turn_re * im + turn_im * re).astype(jnp.bfloat16),
    )


def dot32(form, left, right):
    return jnp.einsum(form, left, right, preferred_element_type=jnp.float32)


def convolve(signal, kernel):
    channels = signal.shape[1]
    filters = kernel.shape[1]
    (outer_re, outer_im), (inner_re, inner_im), (turn_re, turn_im) = tables()
    outer = jnp.asarray(np.concatenate([outer_re, outer_im]), jnp.bfloat16)
    forward = jnp.asarray(np.block([[inner_re, inner_im], [-inner_im, inner_re]]), jnp.bfloat16)
    inverse = jnp.asarray(np.block([[inner_re, -inner_im], [inner_im, inner_re]]), jnp.bfloat16)
    turn_re = turn_re[:, None, :]
    turn_im = turn_im[:, None, :]
    data = jnp.concatenate([signal, kernel], axis=1)
    first = dot32("ka,acb->kcb", outer, data).astype(jnp.bfloat16).astype(jnp.float32)
    turned = rotate(turn_re, turn_im, first[:ROWS], first[ROWS:])
    spec = dot32("kcb,bq->kcq", jnp.concatenate(turned, axis=2), forward)
    spec_re, spec_im = spec[..., :BLOCK], spec[..., BLOCK:]
    filt_re = jnp.repeat(spec_re[:, channels:], channels // filters, axis=1)
    filt_im = jnp.repeat(spec_im[:, channels:], channels // filters, axis=1)
    weighted = rotate(filt_re, filt_im, spec_re[:, :channels], spec_im[:, :channels])
    back = dot32("kcq,qb->kcb", jnp.concatenate(weighted, axis=2), inverse)
    unturned = rotate(turn_re, -turn_im, back[..., :BLOCK], back[..., BLOCK:])
    fold = np.full((ROWS, 1), 2.0, np.float32)
    fold[0] = fold[-1] = 1.0
    final = jnp.asarray(np.concatenate([outer_re * fold, outer_im * fold]), jnp.bfloat16)
    conv = dot32("ka,kcb->acb", final, jnp.concatenate(unturned, axis=0))
    return (conv * (1.0 / TOTAL)).astype(jnp.bfloat16)


def local(section_input, long_filter, short_filter, skip_gain):
    acts_local = section_input[0]
    tok_rows, chan_local = acts_local.shape
    filt_local = long_filter.shape[2]
    n_ctx = lax.axis_size("ctx")
    partial_squares = jnp.sum(acts_local * acts_local, axis=1)
    total_squares = lax.psum(partial_squares, "tp")
    normed = (acts_local * lax.rsqrt(total_squares / CHAN + 1e-06)[:, None]).astype(jnp.bfloat16)
    earlier = from_behind(normed[tok_rows - (TAPS - 1) :], "ctx", 1)
    extended = jnp.concatenate([earlier, normed], axis=0)
    taps_all = short_filter[0].astype(jnp.float32)
    featured = []
    for feature_id in range(3):
        running = jnp.zeros((tok_rows, chan_local), jnp.float32)
        for offset in range(TAPS):
            begin_row = TAPS - 1 - offset
            running = (
                running
                + taps_all[feature_id, offset][None, :] * extended[begin_row : begin_row + tok_rows]
            )
        featured.append(running)
    query = featured[0].astype(jnp.bfloat16)
    product = (featured[1] * featured[2]).astype(jnp.bfloat16)
    signal = product.T.reshape(n_ctx, chan_local // n_ctx, BLOCK)
    kernel = long_filter[0].T.reshape(n_ctx, filt_local // n_ctx, BLOCK)
    signal = lax.all_to_all(signal, "ctx", split_axis=0, concat_axis=0, tiled=True)
    kernel = lax.all_to_all(kernel, "ctx", split_axis=0, concat_axis=0, tiled=True)
    conv = convolve(signal, kernel)
    conv = lax.all_to_all(conv, "ctx", split_axis=0, concat_axis=0, tiled=True)
    conv_tokens = conv.reshape(chan_local, BLOCK).T
    finished = acts_local + query.astype(jnp.float32) * (
        conv_tokens.astype(jnp.float32) + skip_gain[0][None, :] * product.astype(jnp.float32)
    )
    received = passed_along(finished.astype(jnp.bfloat16), "section", 1).astype(finished.dtype)
    return received[None]


def solution(mesh):
    in_specs = (
        P("section", "ctx", "tp"),
        P("section", "ctx", "tp"),
        P("section", None, None, "tp"),
        P("section", "tp"),
    )
    out_specs = P("section", "ctx", "tp")
    return jax.shard_map(local, mesh=mesh, in_specs=in_specs, out_specs=out_specs, check_vma=False)
```

```python
import functools

import jax
import jax.numpy as jnp
import numpy as np
from jax import lax
from jax.experimental import pallas as pl
from jax.experimental.pallas import tpu as pltpu
from jax.sharding import PartitionSpec as P

CHAN = 4096
TAPS = 3
BLOCK = 128
SEQ = 8192
HALF = SEQ // BLOCK
SPAN = 2 * HALF
TOTAL = SPAN * BLOCK
ROWS = HALF + 1
PAD = 80
SIDE = 8
TOGETHER = 4
MESH = pl.DeviceIdType.MESH


def unit_pair(position, period):
    mirror = period - position
    folded = np.minimum(position, mirror)
    angle = folded.astype(np.float32) * np.float32(2 * np.pi / period)
    cosine = np.where(4 * folded == period, 0.0, np.cos(angle)).astype(np.float32)
    sine = np.where((folded == 0) | (2 * folded == period), 0.0, np.sin(angle)).astype(np.float32)
    sine = np.where(position > mirror, -sine, sine)
    return cosine, -sine


def padded(rows):
    return np.pad(rows, ((0, PAD - ROWS), (0, 0)))


def tables():
    k1 = np.arange(ROWS)
    a = np.arange(HALF)
    b = np.arange(BLOCK)
    outer_re, outer_im = unit_pair(k1[:, None] * a[None, :] % SPAN, SPAN)
    inner_re, inner_im = unit_pair(b[:, None] * b[None, :] % BLOCK, BLOCK)
    turn_re, turn_im = unit_pair(k1[:, None] * b[None, :] % TOTAL, TOTAL)
    fold = np.full((ROWS, 1), 2.0 / TOTAL, np.float32)
    fold[0] = fold[-1] = 1.0 / TOTAL
    outer = jnp.asarray(np.concatenate([padded(outer_re), padded(outer_im)]), jnp.bfloat16)
    forward = jnp.asarray(np.block([[inner_re, inner_im], [-inner_im, inner_re]]), jnp.bfloat16)
    inverse = jnp.asarray(np.block([[inner_re, -inner_im], [inner_im, inner_re]]), jnp.bfloat16)
    turn = jnp.asarray(np.stack([padded(turn_re), padded(turn_im)]), jnp.float32)
    rounded = [padded(np.asarray(t.astype(jnp.bfloat16)).astype(np.float32) * fold) for t in (outer_re, outer_im)]
    final = jnp.asarray(np.concatenate(rounded).T, jnp.bfloat16)
    return outer, forward, inverse, turn, final


def from_behind(block, axis, distance):
    devices = range(lax.axis_size(axis))
    route = [(i - distance, i) for i in devices if i - distance in devices]
    return lax.ppermute(block, axis, route)


def passed_along(x, axis, by):
    peers = lax.axis_size(axis)
    return lax.ppermute(x, axis, [(i, (i + by) % peers) for i in range(peers)])


def dot32(left, right):
    return lax.dot_general(left, right, (((1,), (0,)), ((), ())), preferred_element_type=jnp.float32)


def transform(slabs, outer, forward, turn):
    first = dot32(outer[...], jnp.concatenate(slabs, axis=1).astype(jnp.bfloat16))
    turned = []
    for j in range(len(slabs)):
        re = first[:PAD, j * BLOCK : (j + 1) * BLOCK]
        im = first[PAD:, j * BLOCK : (j + 1) * BLOCK]
        turned_re = turn[0] * re - turn[1] * im
        turned_im = turn[0] * im + turn[1] * re
        turned.append(jnp.concatenate([turned_re, turned_im], axis=1).astype(jnp.bfloat16))
    return dot32(jnp.concatenate(turned, axis=0), forward[...])


def untransform(spec, count, filt_re, filt_im, inverse, turn, final):
    weighted = []
    for j in range(count):
        re = spec[j * PAD : (j + 1) * PAD, :BLOCK]
        im = spec[j * PAD : (j + 1) * PAD, BLOCK:]
        out_re = re * filt_re - im * filt_im
        out_im = re * filt_im + im * filt_re
        weighted.append(jnp.concatenate([out_re, out_im], axis=1).astype(jnp.bfloat16))
    back = dot32(jnp.concatenate(weighted, axis=0), inverse[...])
    unturned = []
    for j in range(count):
        re = back[j * PAD : (j + 1) * PAD, :BLOCK]
        im = back[j * PAD : (j + 1) * PAD, BLOCK:]
        out_re = turn[0] * re + turn[1] * im
        out_im = turn[0] * im - turn[1] * re
        unturned.append(jnp.concatenate([out_re, out_im], axis=0).astype(jnp.bfloat16))
    return dot32(final[...], jnp.concatenate(unturned, axis=1))


def middle(
    x_ref, f_ref, outer, forward, inverse, turn, final, o_ref,
    got, got_f, wide, wide_f, filt, result, ready,
    met, send_sem, recv_sem, fsend_sem, frecv_sem, bsend_sem, brecv_sem,
):
    peers = HALF
    chans = x_ref.shape[1]
    filters = f_ref.shape[1]
    me = lax.axis_index("ctx")
    z, y = me // SIDE, me % SIDE
    barrier = pltpu.get_barrier_semaphore()
    for k in range(1, SIDE):
        pl.semaphore_signal(barrier, inc=1, device_id={"ctx": z * SIDE + (y + k) % SIDE}, device_id_type=MESH)
        pl.semaphore_signal(barrier, inc=1, device_id={"ctx": (z + k) % SIDE * SIDE + y}, device_id_type=MESH)
    pl.semaphore_wait(barrier, 2 * (SIDE - 1))
    for k in range(1, SIDE):
        pl.semaphore_signal(met, inc=1, device_id={"ctx": (z + k) % SIDE * SIDE + y}, device_id_type=MESH)
    pl.semaphore_wait(met, SIDE - 1)

    def peer(k):
        kk = (k * 27) % peers
        return (z + kk // SIDE) % SIDE * SIDE + (y + kk % SIDE) % SIDE

    def copy(src, dst, send, recv, k):
        to = peer(k)
        return pltpu.make_async_remote_copy(
            src_ref=src.at[to], dst_ref=dst.at[me], send_sem=send.at[k], recv_sem=recv.at[k],
            device_id={"ctx": to}, device_id_type=MESH,
        )

    def start(k, carry):
        copy(f_ref, got_f, fsend_sem, frecv_sem, k).start()
        copy(x_ref, got, send_sem, recv_sem, k).start()
        return carry

    lax.fori_loop(1, peers, start, 0)
    got[me] = x_ref[me]
    got_f[me] = f_ref[me]

    def wait(src, dst, send, recv):
        def body(k, carry):
            copy(src, dst, send, recv, k).wait()
            return carry

        lax.fori_loop(1, peers, body, 0)

    wait(f_ref, got_f, fsend_sem, frecv_sem)
    wide_f[...] = got_f[...].astype(jnp.float32)
    spec = transform([wide_f[:, f, :] for f in range(filters)], outer, forward, turn)
    for f in range(filters):
        filt[f] = spec[f * PAD : (f + 1) * PAD]
    wait(x_ref, got, send_sem, recv_sem)
    wide[...] = got[...].astype(jnp.float32).reshape(wide.shape)

    def group(g, carry):
        at = [g * TOGETHER + j for j in range(TOGETHER)]
        slabs = [wide[pl.ds(c, peers, stride=chans), :] for c in at]
        spec = transform(slabs, outer, forward, turn)
        gain = filt[g * TOGETHER // (chans // filters)]
        conv = untransform(spec, TOGETHER, gain[:, :BLOCK], gain[:, BLOCK:], inverse, turn, final)
        for j, c in enumerate(at):
            result[pl.ds(c, peers, stride=chans), :] = conv[:, j * BLOCK : (j + 1) * BLOCK]
        return carry

    lax.fori_loop(0, chans // TOGETHER, group, 0)
    ready[...] = result[...].reshape(ready.shape).astype(jnp.bfloat16)

    def start_back(k, carry):
        copy(ready, o_ref, bsend_sem, brecv_sem, k).start()
        return carry

    lax.fori_loop(1, peers, start_back, 0)
    o_ref[me] = ready[me]
    wait(ready, o_ref, bsend_sem, brecv_sem)


def convolve(signal, kernel):
    peers, chans, _ = signal.shape
    filters = kernel.shape[1]
    vmem = pl.BlockSpec(memory_space=pltpu.VMEM)
    sems = pltpu.SemaphoreType.DMA((peers,))
    return pl.pallas_call(
        middle,
        out_shape=jax.ShapeDtypeStruct(signal.shape, jnp.bfloat16),
        in_specs=[vmem] * 7,
        out_specs=vmem,
        scratch_shapes=[
            pltpu.VMEM(signal.shape, jnp.bfloat16),
            pltpu.VMEM(kernel.shape, jnp.bfloat16),
            pltpu.VMEM((peers * chans, BLOCK), jnp.float32),
            pltpu.VMEM(kernel.shape, jnp.float32),
            pltpu.VMEM((filters, PAD, 2 * BLOCK), jnp.float32),
            pltpu.VMEM((peers * chans, BLOCK), jnp.float32),
            pltpu.VMEM(signal.shape, jnp.bfloat16),
            pltpu.SemaphoreType.REGULAR,
        ]
        + [sems] * 6,
        compiler_params=pltpu.CompilerParams(collective_id=0, has_side_effects=True, vmem_limit_bytes=48 << 20),
        name="middle",
    )(signal, kernel, *tables())


def local(section_input, long_filter, short_filter, skip_gain):
    acts_local = section_input[0]
    tok_rows, chan_local = acts_local.shape
    filt_local = long_filter.shape[2]
    n_ctx = lax.axis_size("ctx")
    partial_squares = jnp.sum(acts_local * acts_local, axis=1)
    total_squares = lax.psum(partial_squares, "tp")
    normed = (acts_local * lax.rsqrt(total_squares / CHAN + 1e-06)[:, None]).astype(jnp.bfloat16)
    earlier = from_behind(normed[tok_rows - (TAPS - 1) :], "ctx", 1)
    extended = jnp.concatenate([earlier, normed], axis=0)
    taps_all = short_filter[0].astype(jnp.float32)
    featured = []
    for feature_id in range(3):
        running = jnp.zeros((tok_rows, chan_local), jnp.float32)
        for offset in range(TAPS):
            begin_row = TAPS - 1 - offset
            running = (
                running
                + taps_all[feature_id, offset][None, :] * extended[begin_row : begin_row + tok_rows]
            )
        featured.append(running)
    query = featured[0].astype(jnp.bfloat16)
    product = (featured[1] * featured[2]).astype(jnp.bfloat16)
    signal = product.T.reshape(n_ctx, chan_local // n_ctx, BLOCK)
    kernel = long_filter[0].T.reshape(n_ctx, filt_local // n_ctx, BLOCK)
    conv = convolve(signal, kernel)
    conv_tokens = conv.reshape(chan_local, BLOCK).T
    finished = acts_local + query.astype(jnp.float32) * (
        conv_tokens.astype(jnp.float32) + skip_gain[0][None, :] * product.astype(jnp.float32)
    )
    received = passed_along(finished.astype(jnp.bfloat16), "section", 1).astype(finished.dtype)
    return received[None]


def solution(mesh):
    in_specs = (
        P("section", "ctx", "tp"),
        P("section", "ctx", "tp"),
        P("section", None, None, "tp"),
        P("section", "tp"),
    )
    out_specs = P("section", "ctx", "tp")
    return jax.shard_map(local, mesh=mesh, in_specs=in_specs, out_specs=out_specs, check_vma=False)
```

```python
import functools

import jax
import jax.numpy as jnp
import numpy as np
from jax import lax
from jax.experimental import pallas as pl
from jax.experimental.pallas import tpu as pltpu
from jax.sharding import PartitionSpec as P

CHAN = 4096
TAPS = 3
BLOCK = 128
SEQ = 8192
HALF = SEQ // BLOCK
SPAN = 2 * HALF
TOTAL = SPAN * BLOCK
ROWS = HALF + 1
PAD = 80
SIDE = 8
TOGETHER = 4
GROUP = 16
HALVES = 2
HALO = 2
TOP = 8
MESH = pl.DeviceIdType.MESH


def unit_pair(position, period):
    mirror = period - position
    folded = np.minimum(position, mirror)
    angle = folded.astype(np.float32) * np.float32(2 * np.pi / period)
    cosine = np.where(4 * folded == period, 0.0, np.cos(angle)).astype(np.float32)
    sine = np.where((folded == 0) | (2 * folded == period), 0.0, np.sin(angle)).astype(np.float32)
    sine = np.where(position > mirror, -sine, sine)
    return cosine, -sine


def padded(rows):
    return np.pad(rows, ((0, PAD - ROWS), (0, 0)))


def tables():
    k1 = np.arange(ROWS)
    a = np.arange(HALF)
    b = np.arange(BLOCK)
    outer_re, outer_im = unit_pair(k1[:, None] * a[None, :] % SPAN, SPAN)
    inner_re, inner_im = unit_pair(b[:, None] * b[None, :] % BLOCK, BLOCK)
    turn_re, turn_im = unit_pair(k1[:, None] * b[None, :] % TOTAL, TOTAL)
    fold = np.full((ROWS, 1), 2.0 / TOTAL, np.float32)
    fold[0] = fold[-1] = 1.0 / TOTAL
    outer = jnp.asarray(np.concatenate([padded(outer_re), padded(outer_im)]), jnp.bfloat16)
    forward = jnp.asarray(np.block([[inner_re, inner_im], [-inner_im, inner_re]]), jnp.bfloat16)
    inverse = jnp.asarray(np.block([[inner_re, -inner_im], [inner_im, inner_re]]), jnp.bfloat16)
    turn = jnp.asarray(np.stack([padded(turn_re), padded(turn_im)]), jnp.float32)
    rounded = [padded(np.asarray(t.astype(jnp.bfloat16)).astype(np.float32) * fold) for t in (outer_re, outer_im)]
    final = jnp.asarray(np.concatenate(rounded).T, jnp.bfloat16)
    return outer, forward, inverse, turn, final


def dot32(left, right):
    return lax.dot_general(left, right, (((1,), (0,)), ((), ())), preferred_element_type=jnp.float32)


def transform(slabs, outer, forward, turn):
    first = dot32(outer[...], jnp.concatenate(slabs, axis=1).astype(jnp.bfloat16))
    turned = []
    for j in range(len(slabs)):
        re = first[:PAD, j * BLOCK : (j + 1) * BLOCK]
        im = first[PAD:, j * BLOCK : (j + 1) * BLOCK]
        turned_re = turn[0] * re - turn[1] * im
        turned_im = turn[0] * im + turn[1] * re
        turned.append(jnp.concatenate([turned_re, turned_im], axis=1).astype(jnp.bfloat16))
    return dot32(jnp.concatenate(turned, axis=0), forward[...])


def untransform(spec, count, filt_re, filt_im, inverse, turn, final):
    weighted = []
    for j in range(count):
        re = spec[j * PAD : (j + 1) * PAD, :BLOCK]
        im = spec[j * PAD : (j + 1) * PAD, BLOCK:]
        out_re = re * filt_re - im * filt_im
        out_im = re * filt_im + im * filt_re
        weighted.append(jnp.concatenate([out_re, out_im], axis=1).astype(jnp.bfloat16))
    back = dot32(jnp.concatenate(weighted, axis=0), inverse[...])
    unturned = []
    for j in range(count):
        re = back[j * PAD : (j + 1) * PAD, :BLOCK]
        im = back[j * PAD : (j + 1) * PAD, BLOCK:]
        out_re = turn[0] * re + turn[1] * im
        out_im = turn[0] * im - turn[1] * re
        unturned.append(jnp.concatenate([out_re, out_im], axis=0).astype(jnp.bfloat16))
    return dot32(final[...], jnp.concatenate(unturned, axis=1))


def tick(
    x_hbm, filter_hbm, short_hbm, skip_hbm, outer_hbm, forward_hbm, inverse_hbm, turn_hbm, final_hbm, o_ref,
    x, kern, short, skip, outer, forward, inverse, turn, final,
    edge, halo, squares, other_squares, taps, normed, query, kern_out, kern_in, kern_wide, filt,
    product, got, wide, result, ready, conv, finished,
    met, load_sem, edge_send, edge_recv, sq_send, sq_recv, kern_send, kern_recv,
    prod_send, prod_recv, conv_send, conv_recv, hop_send, hop_recv,
):
    rows, chans = x.shape
    half_chans = chans // HALVES
    section, ctx, tp = lax.axis_index("section"), lax.axis_index("ctx"), lax.axis_index("tp")
    n_section = lax.axis_size("section")
    z, y = ctx // SIDE, ctx % SIDE
    following, before = (ctx + 1) % HALF, (ctx + HALF - 1) % HALF

    pairs = (
        (x_hbm, x), (filter_hbm, kern), (short_hbm, short), (skip_hbm, skip), (outer_hbm, outer),
        (forward_hbm, forward), (inverse_hbm, inverse), (turn_hbm, turn), (final_hbm, final),
    )
    loads = [pltpu.make_async_copy(src, dst, load_sem.at[i]) for i, (src, dst) in enumerate(pairs)]
    for load in loads:
        load.start()

    barrier = pltpu.get_barrier_semaphore()

    def greet(sem, **to):
        pl.semaphore_signal(sem, inc=1, device_id=to, device_id_type=MESH)

    greet(barrier, tp=1 - tp)
    greet(barrier, ctx=before, tp=0)
    greet(barrier, ctx=before, tp=1)
    for k in range(1, SIDE):
        greet(barrier, ctx=(z + k) % SIDE * SIDE + y)
        greet(barrier, ctx=z * SIDE + (y + k) % SIDE)
    greet(barrier, section=(section + n_section - 1) % n_section)

    loads[0].wait()
    edge[...] = x[rows - HALO :, :]
    total = jnp.zeros((rows, BLOCK), jnp.float32)
    for j in range(chans // BLOCK):
        part = x[:, j * BLOCK : (j + 1) * BLOCK]
        total = total + part * part
    squares[...] = total
    pl.semaphore_wait(barrier, 2 * (SIDE - 1) + 4)
    for k in range(1, SIDE):
        greet(met, ctx=(z + k) % SIDE * SIDE + y)

    def remote(src, dst, send, recv, **to):
        return pltpu.make_async_remote_copy(
            src_ref=src, dst_ref=dst, send_sem=send, recv_sem=recv, device_id=to, device_id_type=MESH
        )

    swap = remote(squares, other_squares, sq_send, sq_recv, tp=1 - tp)
    swap.start()
    edges = [
        remote(edge, halo.at[0], edge_send.at[0], edge_recv.at[0], ctx=following),
        remote(edge, halo.at[1], edge_send.at[1], edge_recv.at[1], ctx=following, tp=1 - tp),
    ]
    for send in edges:
        send.start()

    for load in loads[1:]:
        load.wait()
    kern_rows = kern[...].astype(jnp.float32).T
    for h in range(HALVES):
        kern_out[:, h, :] = kern_rows[h * HALF : (h + 1) * HALF]
    for f in range(3):
        taps[f] = short[f].astype(jnp.float32)
    pl.semaphore_wait(met, SIDE - 1)

    def at(dz, dy):
        return (z + dz) % SIDE * SIDE + (y + dy) % SIDE

    def send_kern(k, carry):
        to = at(k // SIDE, k % SIDE)
        remote(kern_out.at[to], kern_in.at[ctx], kern_send, kern_recv, ctx=to).start()
        return carry

    lax.fori_loop(1, HALF, send_kern, 0)
    pltpu.make_async_copy(kern_out.at[ctx], kern_in.at[ctx], kern_recv).start()

    swap.wait()
    mean = jnp.sum(squares[...] + other_squares[...], axis=1, keepdims=True) / CHAN
    scale = lax.rsqrt(mean + 1e-06)
    for j in range(chans // BLOCK):
        lanes = slice(j * BLOCK, (j + 1) * BLOCK)
        normed[TOP:, lanes] = (x[:, lanes] * scale).astype(jnp.bfloat16).astype(jnp.float32)
    for send in edges:
        send.wait()
    mine, theirs = halo[0], halo[1]
    edge_mean = (
        jnp.sum(mine * mine, axis=1, keepdims=True) + jnp.sum(theirs * theirs, axis=1, keepdims=True)
    ) / CHAN
    edge_normed = (mine * lax.rsqrt(edge_mean + 1e-06)).astype(jnp.bfloat16).astype(jnp.float32)
    normed[TOP - HALO : TOP, :] = jnp.where(ctx == 0, 0.0, edge_normed)

    for h in range(HALVES):

        def chunk(i, carry):
            dz = i * 3 % SIDE
            row = (z + dz) % SIDE
            lanes = pl.ds(pl.multiple_of(h * half_chans + row * BLOCK, BLOCK), BLOCK)
            shifted = [normed[pl.ds(TOP - t, rows), lanes] for t in range(TAPS)]
            features = []
            for f in range(3):
                running = taps[f, pl.ds(0, 1), lanes] * shifted[0]
                for t in range(1, TAPS):
                    running = running + taps[f, pl.ds(t, 1), lanes] * shifted[t]
                features.append(running)
            ask = features[0].astype(jnp.bfloat16).astype(jnp.float32)
            gated = (features[1] * features[2]).astype(jnp.bfloat16).astype(jnp.float32)
            query[:, lanes] = ask
            x[:, lanes] = x[:, lanes] + ask * (skip[:, lanes] * gated)
            product[h, pl.ds(row * SIDE, SIDE)] = gated.T.astype(jnp.bfloat16).reshape(SIDE, GROUP, BLOCK)

            def send(r, inner):
                to = row * SIDE + (y + r) % SIDE
                remote(product.at[h, to], got.at[h, ctx], prod_send.at[h], prod_recv.at[h], ctx=to).start()
                return inner

            lax.fori_loop(jnp.where(i == 0, 1, 0), SIDE, send, 0)
            return carry

        lax.fori_loop(0, SIDE, chunk, 0)
        pltpu.make_async_copy(product.at[h, ctx], got.at[h, ctx], prod_recv.at[h]).start()

    def wait_in(dst, sem):
        pltpu.make_async_copy(dst, dst, sem).wait()

    wait_in(kern_in, kern_recv)
    kern_wide[...] = kern_in[...]
    spec = transform([kern_wide[:, h, :] for h in range(HALVES)], outer, forward, turn)
    for h in range(HALVES):
        filt[h] = spec[h * PAD : (h + 1) * PAD]

    for h in range(HALVES):
        wait_in(got.at[h], prod_recv.at[h])
        wide[...] = got[h].astype(jnp.float32).reshape(wide.shape)

        def group(g, carry):
            ids = [g * TOGETHER + j for j in range(TOGETHER)]
            slabs = [wide[pl.ds(c, HALF, stride=GROUP), :] for c in ids]
            spec = transform(slabs, outer, forward, turn)
            gain = filt[h]
            out = untransform(spec, TOGETHER, gain[:, :BLOCK], gain[:, BLOCK:], inverse, turn, final)
            for j, c in enumerate(ids):
                result[pl.ds(c, HALF, stride=GROUP), :] = out[:, j * BLOCK : (j + 1) * BLOCK]
            return carry

        lax.fori_loop(0, GROUP // TOGETHER, group, 0)
        ready[h] = result[...].reshape(HALF, GROUP, BLOCK).astype(jnp.bfloat16)

        def send_back(k, carry):
            to = at(k // SIDE * 3 % SIDE, k % SIDE)
            remote(ready.at[h, to], conv.at[h, ctx], conv_send.at[h], conv_recv.at[h, z], ctx=to).start()
            return carry

        lax.fori_loop(1, HALF, send_back, 0)
        pltpu.make_async_copy(ready.at[h, ctx], conv.at[h, ctx], conv_recv.at[h, z]).start()

    onward = (section + 1) % n_section
    for h in range(HALVES):

        def finish(i, carry):
            row = (z + SIDE - i * 3 % SIDE) % SIDE
            blocks = pl.ds(row * SIDE, SIDE)
            lanes = pl.ds(pl.multiple_of(h * half_chans + row * BLOCK, BLOCK), BLOCK)
            wait_in(conv.at[h, blocks], conv_recv.at[h, row])
            got_conv = conv[h, blocks].astype(jnp.float32).reshape(BLOCK, BLOCK).T
            finished[:, lanes] = (x[:, lanes] + query[:, lanes] * got_conv).astype(jnp.bfloat16)
            remote(finished.at[:, lanes], o_ref.at[:, lanes], hop_send, hop_recv, section=onward).start()
            return carry

        lax.fori_loop(0, SIDE, finish, 0)

    remote(finished, o_ref, hop_send, hop_recv, section=onward).wait()
    sent = pl.ds(0, HALF - 1)
    pltpu.make_async_copy(kern_out.at[sent], kern_out.at[sent], kern_send).wait()
    for h in range(HALVES):
        wait_in(product.at[h, sent], prod_send.at[h])
        wait_in(ready.at[h, sent], conv_send.at[h])


def local(section_input, long_filter, short_filter, skip_gain):
    rows, chans = section_input.shape[1:]
    args = (section_input[0], long_filter[0], short_filter[0], skip_gain, *tables())
    anywhere = pl.BlockSpec(memory_space=pl.ANY)
    half_blocks = (HALVES, HALF, GROUP, BLOCK)
    f32, bf16 = jnp.float32, jnp.bfloat16
    dma = pltpu.SemaphoreType.DMA
    scratch = [pltpu.VMEM(arg.shape, arg.dtype) for arg in args] + [
        pltpu.VMEM((HALO, chans), f32),
        pltpu.VMEM((2, HALO, chans), f32),
        pltpu.VMEM((rows, BLOCK), f32),
        pltpu.VMEM((rows, BLOCK), f32),
        pltpu.VMEM((3, TAPS, chans), f32),
        pltpu.VMEM((TOP + rows, chans), f32),
        pltpu.VMEM((rows, chans), f32),
        pltpu.VMEM((HALF, HALVES, BLOCK), f32),
        pltpu.VMEM((HALF, HALVES, BLOCK), f32),
        pltpu.VMEM((HALF, HALVES, BLOCK), f32),
        pltpu.VMEM((HALVES, PAD, 2 * BLOCK), f32),
        pltpu.VMEM(half_blocks, bf16),
        pltpu.VMEM(half_blocks, bf16),
        pltpu.VMEM((HALF * GROUP, BLOCK), f32),
        pltpu.VMEM((HALF * GROUP, BLOCK), f32),
        pltpu.VMEM(half_blocks, bf16),
        pltpu.VMEM(half_blocks, bf16),
        pltpu.VMEM((rows, chans), bf16),
        pltpu.SemaphoreType.REGULAR,
        dma((len(args),)),
        dma((2,)), dma((2,)),
        dma, dma,
        dma, dma,
        dma((HALVES,)), dma((HALVES,)),
        dma((HALVES,)), dma((HALVES, SIDE)),
        dma, dma,
    ]
    received = pl.pallas_call(
        tick,
        out_shape=jax.ShapeDtypeStruct((rows, chans), bf16),
        in_specs=[anywhere] * len(args),
        out_specs=pl.BlockSpec(memory_space=pltpu.VMEM),
        scratch_shapes=scratch,
        compiler_params=pltpu.CompilerParams(collective_id=0, has_side_effects=True, vmem_limit_bytes=48 << 20),
        name="tick",
    )(*args)
    return received.astype(section_input.dtype)[None]


def solution(mesh):
    in_specs = (
        P("section", "ctx", "tp"),
        P("section", "ctx", "tp"),
        P("section", None, None, "tp"),
        P("section", "tp"),
    )
    out_specs = P("section", "ctx", "tp")
    return jax.shard_map(local, mesh=mesh, in_specs=in_specs, out_specs=out_specs, check_vma=False)
```

```python
import functools

import jax
import jax.numpy as jnp
import numpy as np
from jax import lax
from jax.experimental import pallas as pl
from jax.experimental.pallas import tpu as pltpu
from jax.sharding import PartitionSpec as P

CHAN = 4096
TAPS = 3
BLOCK = 128
SEQ = 8192
HALF = SEQ // BLOCK
SPAN = 2 * HALF
TOTAL = SPAN * BLOCK
ROWS = HALF + 1
PAD = 80
SIDE = 8
TOGETHER = 4
GROUP = 16
HALVES = 2
HALO = 2
TOP = 8
MESH = pl.DeviceIdType.MESH


def unit_pair(position, period):
    mirror = period - position
    folded = np.minimum(position, mirror)
    angle = folded.astype(np.float32) * np.float32(2 * np.pi / period)
    cosine = np.where(4 * folded == period, 0.0, np.cos(angle)).astype(np.float32)
    sine = np.where((folded == 0) | (2 * folded == period), 0.0, np.sin(angle)).astype(np.float32)
    sine = np.where(position > mirror, -sine, sine)
    return cosine, -sine


def padded(rows):
    return np.pad(rows, ((0, PAD - ROWS), (0, 0)))


def tables():
    k1 = np.arange(ROWS)
    a = np.arange(HALF)
    b = np.arange(BLOCK)
    outer_re, outer_im = unit_pair(k1[:, None] * a[None, :] % SPAN, SPAN)
    inner_re, inner_im = unit_pair(b[:, None] * b[None, :] % BLOCK, BLOCK)
    turn_re, turn_im = unit_pair(k1[:, None] * b[None, :] % TOTAL, TOTAL)
    fold = np.full((ROWS, 1), 2.0 / TOTAL, np.float32)
    fold[0] = fold[-1] = 1.0 / TOTAL
    outer = jnp.asarray(np.concatenate([padded(outer_re), padded(outer_im)]), jnp.bfloat16)
    forward = jnp.asarray(np.block([[inner_re, inner_im], [-inner_im, inner_re]]), jnp.bfloat16)
    inverse = jnp.asarray(np.block([[inner_re, -inner_im], [inner_im, inner_re]]), jnp.bfloat16)
    turn = jnp.asarray(np.stack([padded(turn_re), padded(turn_im)]), jnp.float32)
    rounded = [padded(np.asarray(t.astype(jnp.bfloat16)).astype(np.float32) * fold) for t in (outer_re, outer_im)]
    final = jnp.asarray(np.concatenate(rounded).T, jnp.bfloat16)
    return outer, forward, inverse, turn, final


def dot32(left, right):
    return lax.dot_general(left, right, (((1,), (0,)), ((), ())), preferred_element_type=jnp.float32)


def transform(slabs, outer, forward, turn):
    first = dot32(outer[...], jnp.concatenate(slabs, axis=1).astype(jnp.bfloat16))
    turned = []
    for j in range(len(slabs)):
        re = first[:PAD, j * BLOCK : (j + 1) * BLOCK]
        im = first[PAD:, j * BLOCK : (j + 1) * BLOCK]
        turned_re = turn[0] * re - turn[1] * im
        turned_im = turn[0] * im + turn[1] * re
        turned.append(jnp.concatenate([turned_re, turned_im], axis=1).astype(jnp.bfloat16))
    return dot32(jnp.concatenate(turned, axis=0), forward[...])


def untransform(spec, count, filt_re, filt_im, inverse, turn, final):
    weighted = []
    for j in range(count):
        re = spec[j * PAD : (j + 1) * PAD, :BLOCK]
        im = spec[j * PAD : (j + 1) * PAD, BLOCK:]
        out_re = re * filt_re - im * filt_im
        out_im = re * filt_im + im * filt_re
        weighted.append(jnp.concatenate([out_re, out_im], axis=1).astype(jnp.bfloat16))
    back = dot32(jnp.concatenate(weighted, axis=0), inverse[...])
    unturned = []
    for j in range(count):
        re = back[j * PAD : (j + 1) * PAD, :BLOCK]
        im = back[j * PAD : (j + 1) * PAD, BLOCK:]
        out_re = turn[0] * re + turn[1] * im
        out_im = turn[0] * im - turn[1] * re
        unturned.append(jnp.concatenate([out_re, out_im], axis=0).astype(jnp.bfloat16))
    return dot32(final[...], jnp.concatenate(unturned, axis=1))


def tick(
    x_hbm, filter_hbm, short_hbm, skip_hbm, outer_hbm, forward_hbm, inverse_hbm, turn_hbm, final_hbm, o_ref,
    x, kern, short, skip, outer, forward, inverse, turn, final,
    edge, halo, squares, other_squares, taps, normed, query, kern_out, kern_in, kern_wide, filt,
    product, got, wide, result, ready, conv, finished,
    met, load_sem, edge_send, edge_recv, sq_send, sq_recv, kern_send, kern_recv,
    prod_send, prod_recv, conv_send, conv_recv, hop_send, hop_recv,
):
    rows, chans = x.shape
    half_chans = chans // HALVES
    section, ctx, tp = lax.axis_index("section"), lax.axis_index("ctx"), lax.axis_index("tp")
    n_section = lax.axis_size("section")
    z, y = ctx // SIDE, ctx % SIDE
    following, before = (ctx + 1) % HALF, (ctx + HALF - 1) % HALF

    pairs = (
        (x_hbm, x), (filter_hbm, kern), (short_hbm, short), (skip_hbm, skip), (outer_hbm, outer),
        (forward_hbm, forward), (inverse_hbm, inverse), (turn_hbm, turn), (final_hbm, final),
    )
    loads = [pltpu.make_async_copy(src, dst, load_sem.at[i]) for i, (src, dst) in enumerate(pairs)]
    for load in loads:
        load.start()

    barrier = pltpu.get_barrier_semaphore()

    def greet(sem, **to):
        pl.semaphore_signal(sem, inc=1, device_id=to, device_id_type=MESH)

    greet(barrier, tp=1 - tp)
    greet(barrier, ctx=before, tp=0)
    greet(barrier, ctx=before, tp=1)
    for k in range(1, SIDE):
        greet(barrier, ctx=(z + k) % SIDE * SIDE + y)
        greet(barrier, ctx=z * SIDE + (y + k) % SIDE)
    greet(barrier, section=(section + n_section - 1) % n_section)

    loads[0].wait()
    edge[...] = x[rows - HALO :, :]
    total = jnp.zeros((rows, BLOCK), jnp.float32)
    for j in range(chans // BLOCK):
        part = x[:, j * BLOCK : (j + 1) * BLOCK]
        total = total + part * part
    squares[...] = total
    pl.semaphore_wait(barrier, 2 * (SIDE - 1) + 4)
    for k in range(1, SIDE):
        greet(met, ctx=(z + k) % SIDE * SIDE + y)

    def remote(src, dst, send, recv, **to):
        return pltpu.make_async_remote_copy(
            src_ref=src, dst_ref=dst, send_sem=send, recv_sem=recv, device_id=to, device_id_type=MESH
        )

    swap = remote(squares, other_squares, sq_send, sq_recv, tp=1 - tp)
    swap.start()
    edges = [
        remote(edge, halo.at[0], edge_send.at[0], edge_recv.at[0], ctx=following),
        remote(edge, halo.at[1], edge_send.at[1], edge_recv.at[1], ctx=following, tp=1 - tp),
    ]
    for send in edges:
        send.start()

    for load in loads[1:]:
        load.wait()
    kern_rows = kern[...].astype(jnp.float32).T
    for h in range(HALVES):
        kern_out[:, h, :] = kern_rows[h * HALF : (h + 1) * HALF]
    for f in range(3):
        taps[f] = short[f].astype(jnp.float32)
    pl.semaphore_wait(met, SIDE - 1)

    def at(dz, dy):
        return (z + dz) % SIDE * SIDE + (y + dy) % SIDE

    def send_kern(k, carry):
        to = at(k // SIDE, k % SIDE)
        remote(kern_out.at[to], kern_in.at[ctx], kern_send, kern_recv, ctx=to).start()
        return carry

    lax.fori_loop(1, HALF, send_kern, 0)
    pltpu.make_async_copy(kern_out.at[ctx], kern_in.at[ctx], kern_recv).start()

    swap.wait()
    mean = jnp.sum(squares[...] + other_squares[...], axis=1, keepdims=True) / CHAN
    scale = lax.rsqrt(mean + 1e-06)
    for j in range(chans // BLOCK):
        lanes = slice(j * BLOCK, (j + 1) * BLOCK)
        normed[TOP:, lanes] = (x[:, lanes] * scale).astype(jnp.bfloat16).astype(jnp.float32)
    for send in edges:
        send.wait()
    mine, theirs = halo[0], halo[1]
    edge_mean = (
        jnp.sum(mine * mine, axis=1, keepdims=True) + jnp.sum(theirs * theirs, axis=1, keepdims=True)
    ) / CHAN
    edge_normed = (mine * lax.rsqrt(edge_mean + 1e-06)).astype(jnp.bfloat16).astype(jnp.float32)
    normed[TOP - HALO : TOP, :] = jnp.where(ctx == 0, 0.0, edge_normed)

    for h in range(HALVES):

        def chunk(i, carry):
            dz = i * 3 % SIDE
            row = (z + dz) % SIDE
            lanes = pl.ds(pl.multiple_of(h * half_chans + row * BLOCK, BLOCK), BLOCK)
            shifted = [normed[pl.ds(TOP - t, rows), lanes] for t in range(TAPS)]
            features = []
            for f in range(3):
                running = taps[f, pl.ds(0, 1), lanes] * shifted[0]
                for t in range(1, TAPS):
                    running = running + taps[f, pl.ds(t, 1), lanes] * shifted[t]
                features.append(running)
            ask = features[0].astype(jnp.bfloat16).astype(jnp.float32)
            gated = (features[1] * features[2]).astype(jnp.bfloat16).astype(jnp.float32)
            query[:, lanes] = ask
            x[:, lanes] = x[:, lanes] + ask * (skip[:, lanes] * gated)
            product[h, pl.ds(row * SIDE, SIDE)] = gated.T.astype(jnp.bfloat16).reshape(SIDE, GROUP, BLOCK)

            def send(r, inner):
                to = row * SIDE + (y + r) % SIDE
                remote(product.at[h, to], got.at[h, ctx], prod_send.at[h], prod_recv.at[h], ctx=to).start()
                return inner

            lax.fori_loop(jnp.where(i == 0, 1, 0), SIDE, send, 0)
            return carry

        lax.fori_loop(0, SIDE, chunk, 0)
        pltpu.make_async_copy(product.at[h, ctx], got.at[h, ctx], prod_recv.at[h]).start()

    def wait_in(dst, sem):
        pltpu.make_async_copy(dst, dst, sem).wait()

    wait_in(kern_in, kern_recv)
    kern_wide[...] = kern_in[...]
    spec = transform([kern_wide[:, h, :] for h in range(HALVES)], outer, forward, turn)
    for h in range(HALVES):
        filt[h] = spec[h * PAD : (h + 1) * PAD]

    for h in range(HALVES):
        wait_in(got.at[h], prod_recv.at[h])
        wide[...] = got[h].astype(jnp.float32).reshape(wide.shape)

        def group(g, carry):
            ids = [g * TOGETHER + j for j in range(TOGETHER)]
            slabs = [wide[pl.ds(c, HALF, stride=GROUP), :] for c in ids]
            spec = transform(slabs, outer, forward, turn)
            gain = filt[h]
            out = untransform(spec, TOGETHER, gain[:, :BLOCK], gain[:, BLOCK:], inverse, turn, final)
            for j, c in enumerate(ids):
                result[pl.ds(c, HALF, stride=GROUP), :] = out[:, j * BLOCK : (j + 1) * BLOCK]
            return carry

        lax.fori_loop(0, GROUP // TOGETHER, group, 0)
        ready[h] = result[...].reshape(HALF, GROUP, BLOCK).astype(jnp.bfloat16)

        def send_back(k, carry):
            to = at(k // SIDE * 3 % SIDE, k % SIDE)
            remote(ready.at[h, to], conv.at[h, ctx], conv_send.at[h], conv_recv.at[h, z], ctx=to).start()
            return carry

        lax.fori_loop(1, HALF, send_back, 0)
        pltpu.make_async_copy(ready.at[h, ctx], conv.at[h, ctx], conv_recv.at[h, z]).start()

    onward = (section + 1) % n_section
    for h in range(HALVES):

        def finish(i, carry):
            row = (z + SIDE - i * 3 % SIDE) % SIDE
            blocks = pl.ds(row * SIDE, SIDE)
            lanes = pl.ds(pl.multiple_of(h * half_chans + row * BLOCK, BLOCK), BLOCK)
            wait_in(conv.at[h, blocks], conv_recv.at[h, row])
            got_conv = conv[h, blocks].astype(jnp.float32).reshape(BLOCK, BLOCK).T
            finished[:, lanes] = (x[:, lanes] + query[:, lanes] * got_conv).astype(jnp.bfloat16)
            remote(finished.at[:, lanes], o_ref.at[:, lanes], hop_send, hop_recv, section=onward).start()
            return carry

        lax.fori_loop(0, SIDE, finish, 0)

    remote(finished, o_ref, hop_send, hop_recv, section=onward).wait()
    sent = pl.ds(0, HALF - 1)
    pltpu.make_async_copy(kern_out.at[sent], kern_out.at[sent], kern_send).wait()
    for h in range(HALVES):
        wait_in(product.at[h, sent], prod_send.at[h])
        wait_in(ready.at[h, sent], conv_send.at[h])


def local(section_input, long_filter, short_filter, skip_gain):
    rows, chans = section_input.shape[1:]
    args = (section_input[0], long_filter[0], short_filter[0], skip_gain, *tables())
    anywhere = pl.BlockSpec(memory_space=pl.ANY)
    half_blocks = (HALVES, HALF, GROUP, BLOCK)
    f32, bf16 = jnp.float32, jnp.bfloat16
    dma = pltpu.SemaphoreType.DMA
    scratch = [pltpu.VMEM(arg.shape, arg.dtype) for arg in args] + [
        pltpu.VMEM((HALO, chans), f32),
        pltpu.VMEM((2, HALO, chans), f32),
        pltpu.VMEM((rows, BLOCK), f32),
        pltpu.VMEM((rows, BLOCK), f32),
        pltpu.VMEM((3, TAPS, chans), f32),
        pltpu.VMEM((TOP + rows, chans), f32),
        pltpu.VMEM((rows, chans), f32),
        pltpu.VMEM((HALF, HALVES, BLOCK), f32),
        pltpu.VMEM((HALF, HALVES, BLOCK), f32),
        pltpu.VMEM((HALF, HALVES, BLOCK), f32),
        pltpu.VMEM((HALVES, PAD, 2 * BLOCK), f32),
        pltpu.VMEM(half_blocks, bf16),
        pltpu.VMEM(half_blocks, bf16),
        pltpu.VMEM((HALF * GROUP, BLOCK), f32),
        pltpu.VMEM((HALF * GROUP, BLOCK), f32),
        pltpu.VMEM(half_blocks, bf16),
        pltpu.VMEM(half_blocks, bf16),
        pltpu.VMEM((rows, chans), bf16),
        pltpu.SemaphoreType.REGULAR,
        dma((len(args),)),
        dma((2,)), dma((2,)),
        dma, dma,
        dma, dma,
        dma((HALVES,)), dma((HALVES,)),
        dma((HALVES,)), dma((HALVES, SIDE)),
        dma, dma,
    ]
    received = pl.pallas_call(
        tick,
        out_shape=jax.ShapeDtypeStruct((rows, chans), bf16),
        in_specs=[anywhere] * len(args),
        out_specs=pl.BlockSpec(memory_space=pltpu.VMEM),
        scratch_shapes=scratch,
        compiler_params=pltpu.CompilerParams(collective_id=0, has_side_effects=True, vmem_limit_bytes=56 << 20),
        name="tick",
    )(*args)
    return received.astype(section_input.dtype)[None]


def solution(mesh):
    in_specs = (
        P("section", "ctx", "tp"),
        P("section", "ctx", "tp"),
        P("section", None, None, "tp"),
        P("section", "tp"),
    )
    out_specs = P("section", "ctx", "tp")
    return jax.shard_map(local, mesh=mesh, in_specs=in_specs, out_specs=out_specs, check_vma=False)
```

```python
import functools

import jax
import jax.numpy as jnp
import numpy as np
from jax import lax
from jax.experimental import pallas as pl
from jax.experimental.pallas import tpu as pltpu
from jax.sharding import PartitionSpec as P

CHAN = 4096
TAPS = 3
BLOCK = 128
SEQ = 8192
HALF = SEQ // BLOCK
SPAN = 2 * HALF
TOTAL = SPAN * BLOCK
ROWS = HALF + 1
PAD = 80
SIDE = 8
TOGETHER = 8
GROUP = 16
HALVES = 2
HALO = 2
TOP = 16
MESH = pl.DeviceIdType.MESH


def unit_pair(position, period):
    mirror = period - position
    folded = np.minimum(position, mirror)
    angle = folded.astype(np.float32) * np.float32(2 * np.pi / period)
    cosine = np.where(4 * folded == period, 0.0, np.cos(angle)).astype(np.float32)
    sine = np.where((folded == 0) | (2 * folded == period), 0.0, np.sin(angle)).astype(np.float32)
    sine = np.where(position > mirror, -sine, sine)
    return cosine, -sine


def padded(rows):
    return np.pad(rows, ((0, PAD - ROWS), (0, 0)))


def tables():
    k1 = np.arange(ROWS)
    a = np.arange(HALF)
    b = np.arange(BLOCK)
    outer_re, outer_im = unit_pair(k1[:, None] * a[None, :] % SPAN, SPAN)
    inner_re, inner_im = unit_pair(b[:, None] * b[None, :] % BLOCK, BLOCK)
    turn_re, turn_im = unit_pair(k1[:, None] * b[None, :] % TOTAL, TOTAL)
    fold = np.full((ROWS, 1), 2.0 / TOTAL, np.float32)
    fold[0] = fold[-1] = 1.0 / TOTAL
    outer = jnp.asarray(np.concatenate([padded(outer_re), padded(outer_im)]), jnp.bfloat16)
    forward = jnp.asarray(np.block([[inner_re, inner_im], [-inner_im, inner_re]]), jnp.bfloat16)
    inverse = jnp.asarray(np.block([[inner_re, -inner_im], [inner_im, inner_re]]), jnp.bfloat16)
    turn = jnp.asarray(np.stack([padded(turn_re), padded(turn_im)]), jnp.float32)
    rounded = [padded(np.asarray(t.astype(jnp.bfloat16)).astype(np.float32) * fold) for t in (outer_re, outer_im)]
    final = jnp.asarray(np.concatenate(rounded).T, jnp.bfloat16)
    return outer, forward, inverse, turn, final


def dot32(left, right):
    return lax.dot_general(left, right, (((1,), (0,)), ((), ())), preferred_element_type=jnp.float32)


def transform(slabs, outer, forward, turn):
    first = dot32(outer[...], jnp.concatenate(slabs, axis=1).astype(jnp.bfloat16))
    turned = []
    for j in range(len(slabs)):
        re = first[:PAD, j * BLOCK : (j + 1) * BLOCK]
        im = first[PAD:, j * BLOCK : (j + 1) * BLOCK]
        turned_re = turn[0] * re - turn[1] * im
        turned_im = turn[0] * im + turn[1] * re
        turned.append(jnp.concatenate([turned_re, turned_im], axis=1).astype(jnp.bfloat16))
    return dot32(jnp.concatenate(turned, axis=0), forward[...])


def untransform(spec, count, filt_re, filt_im, inverse, turn, final):
    weighted = []
    for j in range(count):
        re = spec[j * PAD : (j + 1) * PAD, :BLOCK]
        im = spec[j * PAD : (j + 1) * PAD, BLOCK:]
        out_re = re * filt_re - im * filt_im
        out_im = re * filt_im + im * filt_re
        weighted.append(jnp.concatenate([out_re, out_im], axis=1).astype(jnp.bfloat16))
    back = dot32(jnp.concatenate(weighted, axis=0), inverse[...])
    unturned = []
    for j in range(count):
        re = back[j * PAD : (j + 1) * PAD, :BLOCK]
        im = back[j * PAD : (j + 1) * PAD, BLOCK:]
        out_re = turn[0] * re + turn[1] * im
        out_im = turn[0] * im - turn[1] * re
        unturned.append(jnp.concatenate([out_re, out_im], axis=0).astype(jnp.bfloat16))
    return dot32(final[...], jnp.concatenate(unturned, axis=1))


def tick(
    x_hbm, filter_hbm, short_hbm, skip_hbm, outer_hbm, forward_hbm, inverse_hbm, turn_hbm, final_hbm, o_hbm,
    x, kern, short, skip, outer, forward, inverse, turn, final,
    edge, halo, edge_squares, halo_squares, squares, other_squares, root, root_in, short_in, skip_in, kern_early,
    taps, normed, moved, moved_in, shifted_in, query, base, kern_out, kern_in, kern_wide, filt,
    product, got, wide, result, ready, conv, finished, finished_in, out,
    met, load_sem, edge_send, edge_recv, sq_send, sq_recv, small_send, small_recv, move_send, move_recv,
    kern_send, kern_recv, prod_send, prod_recv, conv_send, conv_recv, hop_send, hop_recv, out_sem,
):
    rows, chans = x.shape
    part = chans // HALVES
    section, ctx, tp = lax.axis_index("section"), lax.axis_index("ctx"), lax.axis_index("tp")
    n_section = lax.axis_size("section")
    z, y = ctx // SIDE, ctx % SIDE
    following, before = (ctx + 1) % HALF, (ctx + HALF - 1) % HALF
    onward = (section + 1) % n_section

    pairs = (
        (x_hbm, x), (filter_hbm, kern), (short_hbm, short), (skip_hbm, skip), (outer_hbm, outer),
        (forward_hbm, forward), (inverse_hbm, inverse), (turn_hbm, turn), (final_hbm, final),
    )
    loads = [pltpu.make_async_copy(src, dst, load_sem.at[i]) for i, (src, dst) in enumerate(pairs)]
    for load in loads:
        load.start()

    barrier = pltpu.get_barrier_semaphore()

    def greet(sem, **to):
        pl.semaphore_signal(sem, inc=1, device_id=to, device_id_type=MESH)

    greet(barrier, tp=1 - tp)
    greet(barrier, ctx=before, tp=0)
    greet(barrier, ctx=before, tp=1)
    for k in range(1, SIDE):
        greet(barrier, ctx=(z + k) % SIDE * SIDE + y)
        greet(barrier, ctx=z * SIDE + (y + k) % SIDE)
    greet(barrier, section=(section + n_section - 1) % n_section)

    loads[0].wait()
    edge[...] = x[rows - HALO :, :]
    total = jnp.zeros((rows, BLOCK), jnp.float32)
    for j in range(chans // BLOCK):
        piece = x[:, j * BLOCK : (j + 1) * BLOCK]
        total = total + piece * piece
    squares[...] = total
    edge_squares[...] = total[rows - HALO :]
    pl.semaphore_wait(barrier, 2 * (SIDE - 1) + 4)

    def remote(src, dst, send, recv, **to):
        return pltpu.make_async_remote_copy(
            src_ref=src, dst_ref=dst, send_sem=send, recv_sem=recv, device_id=to, device_id_type=MESH
        )

    edges = [
        remote(edge, halo, edge_send.at[0], edge_recv.at[0], ctx=following),
        remote(edge_squares, halo_squares.at[0], edge_send.at[1], edge_recv.at[1], ctx=following),
        remote(edge_squares, halo_squares.at[1], edge_send.at[2], edge_recv.at[2], ctx=following, tp=1 - tp),
    ]
    for send in edges:
        send.start()
    swap = remote(squares, other_squares, sq_send, sq_recv, tp=1 - tp)
    swap.start()
    for k in range(1, SIDE):
        greet(met, ctx=(z + k) % SIDE * SIDE + y)

    for load in loads[1:]:
        load.wait()
    late = pl.ds(part, part)
    smalls = [
        remote(short.at[:, :, late], short_in, small_send.at[0], small_recv.at[0], section=onward),
        remote(skip.at[:, late], skip_in, small_send.at[1], small_recv.at[1], section=onward),
        remote(kern, kern_early, small_send.at[2], small_recv.at[2], section=onward),
        remote(root, root_in, small_send.at[3], small_recv.at[3], section=onward),
    ]
    for send in smalls[:3]:
        send.start()
    for f in range(3):
        taps[0, f] = short[f, :, :part].astype(jnp.float32)

    swap.wait_recv()
    mean = jnp.sum(squares[...] + other_squares[...], axis=1, keepdims=True) / CHAN + 1e-06
    scale = lax.rsqrt(mean)
    for send in edges:
        send.wait_recv()
    edge_mean = jnp.sum(halo_squares[0] + halo_squares[1], axis=1, keepdims=True) / CHAN + 1e-06
    edge_normed = jnp.where(ctx == 0, 0.0, halo[...] * lax.rsqrt(edge_mean))
    normed[TOP - HALO : TOP, :] = edge_normed[:, :part].astype(jnp.bfloat16).astype(jnp.float32)
    edge_late = jnp.concatenate([jnp.zeros((TOP - HALO, part), jnp.float32), edge_normed[:, part:]], axis=0)
    moved[:TOP, :] = edge_late.astype(jnp.bfloat16)
    for j in range(part // BLOCK):
        lanes = slice(part + j * BLOCK, part + (j + 1) * BLOCK)
        moved[TOP:, j * BLOCK : (j + 1) * BLOCK] = (x[:, lanes] * scale).astype(jnp.bfloat16)

    def move(row):
        lanes = pl.ds(pl.multiple_of(row * BLOCK, BLOCK), BLOCK)
        return remote(moved.at[:, lanes], moved_in.at[:, lanes], move_send, move_recv.at[row], section=onward)

    def lane_row(i):
        return (z + i * 3) % SIDE

    def start_move(i, carry):
        move(lane_row(i)).start()
        return carry

    lax.fori_loop(0, SIDE, start_move, 0)
    for j in range(part // BLOCK):
        lanes = slice(j * BLOCK, (j + 1) * BLOCK)
        normed[TOP:, lanes] = (x[:, lanes] * scale).astype(jnp.bfloat16).astype(jnp.float32)
    pl.semaphore_wait(met, SIDE - 1)

    def features(h, lanes, shifted, gain):
        made = []
        for f in range(3):
            running = taps[h, f, pl.ds(0, 1), lanes] * shifted[0]
            for t in range(1, TAPS):
                running = running + taps[h, f, pl.ds(t, 1), lanes] * shifted[t]
            made.append(running)
        ask = made[0].astype(jnp.bfloat16).astype(jnp.float32)
        gated = (made[1] * made[2]).astype(jnp.bfloat16).astype(jnp.float32)
        return ask, gated, ask * (gain * gated)

    def send_products(h, row, gated, first):
        product[h, pl.ds(row * SIDE, SIDE)] = gated.T.astype(jnp.bfloat16).reshape(SIDE, GROUP, BLOCK)

        def send(r, inner):
            to = row * SIDE + (y + r) % SIDE
            remote(product.at[h, to], got.at[h, ctx], prod_send.at[h], prod_recv.at[h], ctx=to).start()
            return inner

        lax.fori_loop(jnp.where(first, 1, 0), SIDE, send, 0)

    def early_chunk(i, carry):
        row = lane_row(i)
        lanes = pl.ds(pl.multiple_of(row * BLOCK, BLOCK), BLOCK)
        shifted = [normed[pl.ds(TOP - t, rows), lanes] for t in range(TAPS)]
        ask, gated, direct = features(0, lanes, shifted, skip[:, lanes])
        query[0, :, lanes] = ask
        base[0, :, lanes] = x[:, lanes] + direct
        send_products(0, row, gated, i == 0)
        return carry

    lax.fori_loop(0, SIDE, early_chunk, 0)
    pltpu.make_async_copy(product.at[0, ctx], got.at[0, ctx], prod_recv.at[0]).start()

    root[...] = jnp.broadcast_to(jnp.sqrt(mean), (rows, BLOCK)).T[:SIDE]
    smalls[3].start()
    smalls[2].wait_recv()
    kern_wide[:, 0, :] = kern[...].astype(jnp.float32).T[:HALF]
    kern_wide[:, 1, :] = kern_early[...].astype(jnp.float32).T[HALF:]
    kern_out[...] = kern_wide[...].astype(jnp.bfloat16)

    def at(dz, dy):
        return (z + dz) % SIDE * SIDE + (y + dy) % SIDE

    def send_kern(k, carry):
        to = at(k // SIDE, k % SIDE)
        remote(kern_out.at[to], kern_in.at[ctx], kern_send, kern_recv, ctx=to).start()
        return carry

    lax.fori_loop(1, HALF, send_kern, 0)
    pltpu.make_async_copy(kern_out.at[ctx], kern_in.at[ctx], kern_recv).start()

    for i in (0, 1, 3):
        smalls[i].wait_recv()
    for f in range(3):
        taps[1, f] = short_in[f].astype(jnp.float32)
    spread = jnp.broadcast_to(root_in[0:1, :], (rows, BLOCK)).T

    def wait_in(dst, sem):
        pltpu.make_async_copy(dst, dst, sem).wait()

    def late_chunk(i, carry):
        row = lane_row(i)
        lanes = pl.ds(pl.multiple_of(row * BLOCK, BLOCK), BLOCK)
        wait_in(moved_in.at[:, lanes], move_recv.at[row])
        shifted_in[...] = moved_in[:, lanes].astype(jnp.float32)
        shifted = [shifted_in[TOP - t : TOP - t + rows, :] for t in range(TAPS)]
        ask, gated, direct = features(1, lanes, shifted, skip_in[:, lanes])
        query[1, :, lanes] = ask
        base[1, :, lanes] = shifted[0] * spread + direct
        send_products(1, row, gated, i == 0)
        return carry

    lax.fori_loop(0, SIDE, late_chunk, 0)
    pltpu.make_async_copy(product.at[1, ctx], got.at[1, ctx], prod_recv.at[1]).start()

    wait_in(kern_in, kern_recv)
    kern_wide[...] = kern_in[...].astype(jnp.float32)
    spec = transform([kern_wide[:, h, :] for h in range(HALVES)], outer, forward, turn)
    for h in range(HALVES):
        filt[h] = spec[h * PAD : (h + 1) * PAD]

    for h in range(HALVES):
        wait_in(got.at[h], prod_recv.at[h])
        wide[...] = got[h].astype(jnp.float32).reshape(wide.shape)

        def group(g, carry):
            ids = [g * TOGETHER + j for j in range(TOGETHER)]
            slabs = [wide[pl.ds(c, HALF, stride=GROUP), :] for c in ids]
            spec = transform(slabs, outer, forward, turn)
            gain = filt[h]
            made = untransform(spec, TOGETHER, gain[:, :BLOCK], gain[:, BLOCK:], inverse, turn, final)
            for j, c in enumerate(ids):
                result[pl.ds(c, HALF, stride=GROUP), :] = made[:, j * BLOCK : (j + 1) * BLOCK]
            return carry

        lax.fori_loop(0, GROUP // TOGETHER, group, 0, unroll=True)
        ready[h] = result[...].reshape(HALF, GROUP, BLOCK).astype(jnp.bfloat16)

        def send_back(k, carry):
            to = at(k // SIDE * 3, k % SIDE)
            remote(ready.at[h, to], conv.at[h, ctx], conv_send.at[h], conv_recv.at[h, z], ctx=to).start()
            return carry

        lax.fori_loop(1, HALF, send_back, 0)
        pltpu.make_async_copy(ready.at[h, ctx], conv.at[h, ctx], conv_recv.at[h, z]).start()

    def finish(h, row, lanes):
        blocks = pl.ds(row * SIDE, SIDE)
        wait_in(conv.at[h, blocks], conv_recv.at[h, row])
        got_conv = conv[h, blocks].astype(jnp.float32).reshape(BLOCK, BLOCK).T
        return base[h, :, lanes] + query[h, :, lanes] * got_conv

    def back_row(i):
        return (z + SIDE - i * 3 % SIDE) % SIDE

    def finish_early(i, carry):
        row = back_row(i)
        lanes = pl.ds(pl.multiple_of(row * BLOCK, BLOCK), BLOCK)
        finished[:, lanes] = finish(0, row, lanes).astype(jnp.bfloat16)
        remote(finished.at[:, lanes], finished_in.at[:, lanes], hop_send, hop_recv.at[row], section=onward).start()
        return carry

    lax.fori_loop(0, SIDE, finish_early, 0)

    def finish_late(i, carry):
        row = back_row(i)
        lanes = pl.ds(pl.multiple_of(row * BLOCK, BLOCK), BLOCK)
        after = pl.ds(pl.multiple_of(part + row * BLOCK, BLOCK), BLOCK)
        wait_in(finished_in.at[:, lanes], hop_recv.at[row])
        out[:, lanes] = finished_in[:, lanes].astype(jnp.float32)
        pltpu.make_async_copy(out.at[:, lanes], o_hbm.at[:, lanes], out_sem).start()
        out[:, after] = finish(1, row, lanes)
        pltpu.make_async_copy(out.at[:, after], o_hbm.at[:, after], out_sem).start()
        return carry

    lax.fori_loop(0, SIDE, finish_late, 0)

    sent = pl.ds(0, HALF - 1)
    for send in (swap, *edges, *smalls):
        send.wait_send()
    wait_in(moved, move_send)
    wait_in(kern_out.at[sent], kern_send)
    for h in range(HALVES):
        wait_in(product.at[h, sent], prod_send.at[h])
        wait_in(ready.at[h, sent], conv_send.at[h])
    wait_in(finished, hop_send)
    pltpu.make_async_copy(out, o_hbm, out_sem).wait()


def local(section_input, long_filter, short_filter, skip_gain):
    rows, chans = section_input.shape[1:]
    part = chans // HALVES
    args = (section_input[0], long_filter[0], short_filter[0], skip_gain, *tables())
    anywhere = pl.BlockSpec(memory_space=pl.ANY)
    f32, bf16 = jnp.float32, jnp.bfloat16
    dma = pltpu.SemaphoreType.DMA
    blocks = pltpu.VMEM((HALVES, HALF, GROUP, BLOCK), bf16)
    kernels = pltpu.VMEM((HALF, HALVES, BLOCK), bf16)
    scratch = [pltpu.VMEM(arg.shape, arg.dtype) for arg in args] + [
        pltpu.VMEM((HALO, chans), f32),
        pltpu.VMEM((HALO, chans), f32),
        pltpu.VMEM((HALO, BLOCK), f32),
        pltpu.VMEM((2, HALO, BLOCK), f32),
        pltpu.VMEM((rows, BLOCK), f32),
        pltpu.VMEM((rows, BLOCK), f32),
        pltpu.VMEM((SIDE, BLOCK), f32),
        pltpu.VMEM((SIDE, BLOCK), f32),
        pltpu.VMEM((3, TAPS, part), bf16),
        pltpu.VMEM((1, part), f32),
        pltpu.VMEM(args[1].shape, bf16),
        pltpu.VMEM((HALVES, 3, TAPS, part), f32),
        pltpu.VMEM((TOP + rows, part), f32),
        pltpu.VMEM((TOP + rows, part), bf16),
        pltpu.VMEM((TOP + rows, part), bf16),
        pltpu.VMEM((TOP + rows, BLOCK), f32),
        pltpu.VMEM((HALVES, rows, part), f32),
        pltpu.VMEM((HALVES, rows, part), f32),
        kernels, kernels, pltpu.VMEM((HALF, HALVES, BLOCK), f32),
        pltpu.VMEM((HALVES, PAD, 2 * BLOCK), f32),
        blocks, blocks,
        pltpu.VMEM((HALF * GROUP, BLOCK), f32),
        pltpu.VMEM((HALF * GROUP, BLOCK), f32),
        blocks, blocks,
        pltpu.VMEM((rows, part), bf16),
        pltpu.VMEM((rows, part), bf16),
        pltpu.VMEM((rows, chans), f32),
        pltpu.SemaphoreType.REGULAR,
        dma((len(args),)),
        dma((3,)), dma((3,)),
        dma, dma,
        dma((4,)), dma((4,)),
        dma, dma((SIDE,)),
        dma, dma,
        dma((HALVES,)), dma((HALVES,)),
        dma((HALVES,)), dma((HALVES, SIDE)),
        dma, dma((SIDE,)),
        dma,
    ]
    received = pl.pallas_call(
        tick,
        out_shape=jax.ShapeDtypeStruct((rows, chans), f32),
        in_specs=[anywhere] * len(args),
        out_specs=anywhere,
        scratch_shapes=scratch,
        compiler_params=pltpu.CompilerParams(collective_id=0, has_side_effects=True, vmem_limit_bytes=56 << 20),
        name="tick",
    )(*args)
    return received[None]


def solution(mesh):
    in_specs = (
        P("section", "ctx", "tp"),
        P("section", "ctx", "tp"),
        P("section", None, None, "tp"),
        P("section", "tp"),
    )
    out_specs = P("section", "ctx", "tp")
    return jax.shard_map(local, mesh=mesh, in_specs=in_specs, out_specs=out_specs, check_vma=False)
```

```python
import functools

import jax
import jax.numpy as jnp
import numpy as np
from jax import lax
from jax.experimental import pallas as pl
from jax.experimental.pallas import tpu as pltpu
from jax.sharding import PartitionSpec as P

CHAN = 4096
TAPS = 3
BLOCK = 128
SEQ = 8192
HALF = SEQ // BLOCK
SPAN = 2 * HALF
TOTAL = SPAN * BLOCK
ROWS = HALF + 1
PAD = 80
SIDE = 8
TOGETHER = 8
GROUP = 16
HALVES = 2
HALO = 2
TOP = 16
MESH = pl.DeviceIdType.MESH


def unit_pair(position, period):
    mirror = period - position
    folded = np.minimum(position, mirror)
    angle = folded.astype(np.float32) * np.float32(2 * np.pi / period)
    cosine = np.where(4 * folded == period, 0.0, np.cos(angle)).astype(np.float32)
    sine = np.where((folded == 0) | (2 * folded == period), 0.0, np.sin(angle)).astype(np.float32)
    sine = np.where(position > mirror, -sine, sine)
    return cosine, -sine


def padded(rows):
    return np.pad(rows, ((0, PAD - ROWS), (0, 0)))


def tables():
    k1 = np.arange(ROWS)
    a = np.arange(HALF)
    b = np.arange(BLOCK)
    outer_re, outer_im = unit_pair(k1[:, None] * a[None, :] % SPAN, SPAN)
    inner_re, inner_im = unit_pair(b[:, None] * b[None, :] % BLOCK, BLOCK)
    turn_re, turn_im = unit_pair(k1[:, None] * b[None, :] % TOTAL, TOTAL)
    fold = np.full((ROWS, 1), 2.0 / TOTAL, np.float32)
    fold[0] = fold[-1] = 1.0 / TOTAL
    outer = jnp.asarray(np.concatenate([padded(outer_re), padded(outer_im)]), jnp.bfloat16)
    forward = jnp.asarray(np.block([[inner_re, inner_im], [-inner_im, inner_re]]), jnp.bfloat16)
    inverse = jnp.asarray(np.block([[inner_re, -inner_im], [inner_im, inner_re]]), jnp.bfloat16)
    turn = jnp.asarray(np.stack([padded(turn_re), padded(turn_im)]), jnp.float32)
    rounded = [padded(np.asarray(t.astype(jnp.bfloat16)).astype(np.float32) * fold) for t in (outer_re, outer_im)]
    final = jnp.asarray(np.concatenate(rounded).T, jnp.bfloat16)
    return outer, forward, inverse, turn, final


def dot32(left, right):
    return lax.dot_general(left, right, (((1,), (0,)), ((), ())), preferred_element_type=jnp.float32)


def transform(slabs, outer, forward, turn):
    first = dot32(outer[...], jnp.concatenate(slabs, axis=1).astype(jnp.bfloat16))
    turned = []
    for j in range(len(slabs)):
        re = first[:PAD, j * BLOCK : (j + 1) * BLOCK]
        im = first[PAD:, j * BLOCK : (j + 1) * BLOCK]
        turned_re = turn[0] * re - turn[1] * im
        turned_im = turn[0] * im + turn[1] * re
        turned.append(jnp.concatenate([turned_re, turned_im], axis=1).astype(jnp.bfloat16))
    return dot32(jnp.concatenate(turned, axis=0), forward[...])


def untransform(spec, count, filt_re, filt_im, inverse, turn, final):
    weighted = []
    for j in range(count):
        re = spec[j * PAD : (j + 1) * PAD, :BLOCK]
        im = spec[j * PAD : (j + 1) * PAD, BLOCK:]
        out_re = re * filt_re - im * filt_im
        out_im = re * filt_im + im * filt_re
        weighted.append(jnp.concatenate([out_re, out_im], axis=1).astype(jnp.bfloat16))
    back = dot32(jnp.concatenate(weighted, axis=0), inverse[...])
    unturned = []
    for j in range(count):
        re = back[j * PAD : (j + 1) * PAD, :BLOCK]
        im = back[j * PAD : (j + 1) * PAD, BLOCK:]
        out_re = turn[0] * re + turn[1] * im
        out_im = turn[0] * im - turn[1] * re
        unturned.append(jnp.concatenate([out_re, out_im], axis=0).astype(jnp.bfloat16))
    return dot32(final[...], jnp.concatenate(unturned, axis=1))


def tick(
    x_hbm, filter_hbm, short_hbm, skip_hbm, outer_hbm, forward_hbm, inverse_hbm, turn_hbm, final_hbm, out,
    x, kern, short, skip, outer, forward, inverse, turn, final,
    edge, halo, edge_squares, halo_squares, squares, other_squares, root, root_in, short_in, skip_in, kern_early,
    taps, normed, moved, moved_in, shifted_in, query, base, kern_out, kern_in, kern_wide, filt,
    product, got, wide, result, ready, conv, finished, finished_in,
    met, load_sem, edge_send, edge_recv, sq_send, sq_recv, small_send, small_recv, move_send, move_recv,
    kern_send, kern_recv, prod_send, prod_recv, conv_send, conv_recv, hop_send, hop_recv,
):
    rows, chans = x.shape
    part = chans // HALVES
    section, ctx, tp = lax.axis_index("section"), lax.axis_index("ctx"), lax.axis_index("tp")
    n_section = lax.axis_size("section")
    z, y = ctx // SIDE, ctx % SIDE
    following, before = (ctx + 1) % HALF, (ctx + HALF - 1) % HALF
    onward = (section + 1) % n_section
    step_z, step_y = 3 + 2 * tp, 3 + 2 * tp

    pairs = (
        (x_hbm, x), (filter_hbm, kern), (short_hbm, short), (skip_hbm, skip), (outer_hbm, outer),
        (forward_hbm, forward), (inverse_hbm, inverse), (turn_hbm, turn), (final_hbm, final),
    )
    loads = [pltpu.make_async_copy(src, dst, load_sem.at[i]) for i, (src, dst) in enumerate(pairs)]
    for load in loads:
        load.start()

    barrier = pltpu.get_barrier_semaphore()

    def greet(sem, **to):
        pl.semaphore_signal(sem, inc=1, device_id=to, device_id_type=MESH)

    greet(barrier, tp=1 - tp)
    greet(barrier, ctx=before, tp=0)
    greet(barrier, ctx=before, tp=1)
    for k in range(1, SIDE):
        greet(barrier, ctx=(z + k) % SIDE * SIDE + y)
        greet(barrier, ctx=z * SIDE + (y + k) % SIDE)
    greet(barrier, section=(section + n_section - 1) % n_section)

    loads[0].wait()
    edge[...] = x[rows - HALO :, :]
    total = jnp.zeros((rows, BLOCK), jnp.float32)
    for j in range(chans // BLOCK):
        piece = x[:, j * BLOCK : (j + 1) * BLOCK]
        total = total + piece * piece
    squares[...] = total
    edge_squares[...] = total[rows - HALO :]
    pl.semaphore_wait(barrier, 2 * (SIDE - 1) + 4)

    def remote(src, dst, send, recv, **to):
        return pltpu.make_async_remote_copy(
            src_ref=src, dst_ref=dst, send_sem=send, recv_sem=recv, device_id=to, device_id_type=MESH
        )

    edges = [
        remote(edge, halo, edge_send.at[0], edge_recv.at[0], ctx=following),
        remote(edge_squares, halo_squares.at[0], edge_send.at[1], edge_recv.at[1], ctx=following),
        remote(edge_squares, halo_squares.at[1], edge_send.at[2], edge_recv.at[2], ctx=following, tp=1 - tp),
    ]
    for send in edges:
        send.start()
    swap = remote(squares, other_squares, sq_send, sq_recv, tp=1 - tp)
    swap.start()
    for k in range(1, SIDE):
        greet(met, ctx=(z + k) % SIDE * SIDE + y)

    for load in loads[1:]:
        load.wait()
    late = pl.ds(part, part)
    smalls = [
        remote(short.at[:, :, late], short_in, small_send.at[0], small_recv.at[0], section=onward),
        remote(skip.at[:, late], skip_in, small_send.at[1], small_recv.at[1], section=onward),
        remote(kern, kern_early, small_send.at[2], small_recv.at[2], section=onward),
        remote(root, root_in, small_send.at[3], small_recv.at[3], section=onward),
    ]
    for send in smalls[:3]:
        send.start()
    for f in range(3):
        taps[0, f] = short[f, :, :part].astype(jnp.float32)

    swap.wait_recv()
    mean = jnp.sum(squares[...] + other_squares[...], axis=1, keepdims=True) / CHAN + 1e-06
    scale = lax.rsqrt(mean)
    for send in edges:
        send.wait_recv()
    edge_mean = jnp.sum(halo_squares[0] + halo_squares[1], axis=1, keepdims=True) / CHAN + 1e-06
    edge_normed = jnp.where(ctx == 0, 0.0, halo[...] * lax.rsqrt(edge_mean))
    normed[TOP - HALO : TOP, :] = edge_normed[:, :part].astype(jnp.bfloat16).astype(jnp.float32)
    edge_late = jnp.concatenate([jnp.zeros((TOP - HALO, part), jnp.float32), edge_normed[:, part:]], axis=0)
    moved[:TOP, :] = edge_late.astype(jnp.bfloat16)
    for j in range(part // BLOCK):
        lanes = slice(part + j * BLOCK, part + (j + 1) * BLOCK)
        moved[TOP:, j * BLOCK : (j + 1) * BLOCK] = (x[:, lanes] * scale).astype(jnp.bfloat16)

    def move(row):
        lanes = pl.ds(pl.multiple_of(row * BLOCK, BLOCK), BLOCK)
        return remote(moved.at[:, lanes], moved_in.at[:, lanes], move_send, move_recv.at[row], section=onward)

    def lane_row(i):
        return (z + i * step_z) % SIDE

    for j in range(part // BLOCK):
        lanes = slice(j * BLOCK, (j + 1) * BLOCK)
        normed[TOP:, lanes] = (x[:, lanes] * scale).astype(jnp.bfloat16).astype(jnp.float32)
    pl.semaphore_wait(met, SIDE - 1)

    def features(h, lanes, shifted, gain):
        made = []
        for f in range(3):
            running = taps[h, f, pl.ds(0, 1), lanes] * shifted[0]
            for t in range(1, TAPS):
                running = running + taps[h, f, pl.ds(t, 1), lanes] * shifted[t]
            made.append(running)
        ask = made[0].astype(jnp.bfloat16).astype(jnp.float32)
        gated = (made[1] * made[2]).astype(jnp.bfloat16).astype(jnp.float32)
        return ask, gated, ask * (gain * gated)

    def send_products(h, row, gated, first):
        product[h, pl.ds(row * SIDE, SIDE)] = gated.T.astype(jnp.bfloat16).reshape(SIDE, GROUP, BLOCK)

        def send(r, inner):
            to = row * SIDE + (y + r * step_y) % SIDE
            remote(product.at[h, to], got.at[h, ctx], prod_send.at[h], prod_recv.at[h], ctx=to).start()
            return inner

        lax.fori_loop(jnp.where(first, 1, 0), SIDE, send, 0)

    def early_chunk(i, carry):
        row = lane_row(i)
        lanes = pl.ds(pl.multiple_of(row * BLOCK, BLOCK), BLOCK)
        shifted = [normed[pl.ds(TOP - t, rows), lanes] for t in range(TAPS)]
        ask, gated, direct = features(0, lanes, shifted, skip[:, lanes])
        query[0, :, lanes] = ask
        base[0, :, lanes] = x[:, lanes] + direct
        move(row).start()
        send_products(0, row, gated, i == 0)
        return carry

    lax.fori_loop(0, SIDE, early_chunk, 0)
    pltpu.make_async_copy(product.at[0, ctx], got.at[0, ctx], prod_recv.at[0]).start()

    root[...] = jnp.broadcast_to(jnp.sqrt(mean), (rows, BLOCK)).T[:SIDE]
    smalls[3].start()
    smalls[2].wait_recv()
    kern_wide[:, 0, :] = kern[...].astype(jnp.float32).T[:HALF]
    kern_wide[:, 1, :] = kern_early[...].astype(jnp.float32).T[HALF:]
    kern_out[...] = kern_wide[...].astype(jnp.bfloat16)

    def at(dz, dy):
        return (z + dz) % SIDE * SIDE + (y + dy) % SIDE

    def send_kern(k, carry):
        to = at(k // SIDE * step_z, k % SIDE * step_y)
        remote(kern_out.at[to], kern_in.at[ctx], kern_send, kern_recv, ctx=to).start()
        return carry

    lax.fori_loop(1, HALF, send_kern, 0)
    pltpu.make_async_copy(kern_out.at[ctx], kern_in.at[ctx], kern_recv).start()

    for i in (0, 1, 3):
        smalls[i].wait_recv()
    for f in range(3):
        taps[1, f] = short_in[f].astype(jnp.float32)
    spread = jnp.broadcast_to(root_in[0:1, :], (rows, BLOCK)).T

    def wait_in(dst, sem):
        pltpu.make_async_copy(dst, dst, sem).wait()

    def late_chunk(i, carry):
        row = lane_row(i)
        lanes = pl.ds(pl.multiple_of(row * BLOCK, BLOCK), BLOCK)
        wait_in(moved_in.at[:, lanes], move_recv.at[row])
        shifted_in[...] = moved_in[:, lanes].astype(jnp.float32)
        shifted = [shifted_in[TOP - t : TOP - t + rows, :] for t in range(TAPS)]
        ask, gated, direct = features(1, lanes, shifted, skip_in[:, lanes])
        query[1, :, lanes] = ask
        base[1, :, lanes] = shifted[0] * spread + direct
        send_products(1, row, gated, i == 0)
        return carry

    lax.fori_loop(0, SIDE, late_chunk, 0)
    pltpu.make_async_copy(product.at[1, ctx], got.at[1, ctx], prod_recv.at[1]).start()

    wait_in(kern_in, kern_recv)
    kern_wide[...] = kern_in[...].astype(jnp.float32)
    spec = transform([kern_wide[:, h, :] for h in range(HALVES)], outer, forward, turn)
    for h in range(HALVES):
        filt[h] = spec[h * PAD : (h + 1) * PAD]

    for h in range(HALVES):
        wait_in(got.at[h], prod_recv.at[h])
        wide[...] = got[h].astype(jnp.float32).reshape(wide.shape)

        def group(g, carry):
            ids = [g * TOGETHER + j for j in range(TOGETHER)]
            slabs = [wide[pl.ds(c, HALF, stride=GROUP), :] for c in ids]
            spec = transform(slabs, outer, forward, turn)
            gain = filt[h]
            made = untransform(spec, TOGETHER, gain[:, :BLOCK], gain[:, BLOCK:], inverse, turn, final)
            for j, c in enumerate(ids):
                result[pl.ds(c, HALF, stride=GROUP), :] = made[:, j * BLOCK : (j + 1) * BLOCK]
            return carry

        lax.fori_loop(0, GROUP // TOGETHER, group, 0, unroll=True)
        ready[h] = result[...].reshape(HALF, GROUP, BLOCK).astype(jnp.bfloat16)

        def send_back(k, carry):
            to = at(k // SIDE * step_z, k % SIDE * step_y)
            remote(ready.at[h, to], conv.at[h, ctx], conv_send.at[h], conv_recv.at[h, z], ctx=to).start()
            return carry

        lax.fori_loop(1, HALF, send_back, 0)
        pltpu.make_async_copy(ready.at[h, ctx], conv.at[h, ctx], conv_recv.at[h, z]).start()

    def finish(h, row, lanes):
        blocks = pl.ds(row * SIDE, SIDE)
        wait_in(conv.at[h, blocks], conv_recv.at[h, row])
        got_conv = conv[h, blocks].astype(jnp.float32).reshape(BLOCK, BLOCK).T
        return base[h, :, lanes] + query[h, :, lanes] * got_conv

    def back_row(i):
        return (z + i * (SIDE - step_z)) % SIDE

    def finish_early(i, carry):
        row = back_row(i)
        lanes = pl.ds(pl.multiple_of(row * BLOCK, BLOCK), BLOCK)
        finished[:, lanes] = finish(0, row, lanes).astype(jnp.bfloat16)
        remote(finished.at[:, lanes], finished_in.at[:, lanes], hop_send, hop_recv.at[row], section=onward).start()
        return carry

    lax.fori_loop(0, SIDE, finish_early, 0)

    def finish_late(i, carry):
        row = back_row(i)
        lanes = pl.ds(pl.multiple_of(row * BLOCK, BLOCK), BLOCK)
        after = pl.ds(pl.multiple_of(part + row * BLOCK, BLOCK), BLOCK)
        wait_in(finished_in.at[:, lanes], hop_recv.at[row])
        out[:, lanes] = finished_in[:, lanes].astype(jnp.float32)
        out[:, after] = finish(1, row, lanes)
        return carry

    lax.fori_loop(0, SIDE, finish_late, 0)

    sent = pl.ds(0, HALF - 1)
    for send in (swap, *edges, *smalls):
        send.wait_send()
    wait_in(moved, move_send)
    wait_in(kern_out.at[sent], kern_send)
    for h in range(HALVES):
        wait_in(product.at[h, sent], prod_send.at[h])
        wait_in(ready.at[h, sent], conv_send.at[h])
    wait_in(finished, hop_send)


def local(section_input, long_filter, short_filter, skip_gain):
    rows, chans = section_input.shape[1:]
    part = chans // HALVES
    args = (section_input[0], long_filter[0], short_filter[0], skip_gain, *tables())
    anywhere = pl.BlockSpec(memory_space=pl.ANY)
    f32, bf16 = jnp.float32, jnp.bfloat16
    dma = pltpu.SemaphoreType.DMA
    blocks = pltpu.VMEM((HALVES, HALF, GROUP, BLOCK), bf16)
    kernels = pltpu.VMEM((HALF, HALVES, BLOCK), bf16)
    scratch = [pltpu.VMEM(arg.shape, arg.dtype) for arg in args] + [
        pltpu.VMEM((HALO, chans), f32),
        pltpu.VMEM((HALO, chans), f32),
        pltpu.VMEM((HALO, BLOCK), f32),
        pltpu.VMEM((2, HALO, BLOCK), f32),
        pltpu.VMEM((rows, BLOCK), f32),
        pltpu.VMEM((rows, BLOCK), f32),
        pltpu.VMEM((SIDE, BLOCK), f32),
        pltpu.VMEM((SIDE, BLOCK), f32),
        pltpu.VMEM((3, TAPS, part), bf16),
        pltpu.VMEM((1, part), f32),
        pltpu.VMEM(args[1].shape, bf16),
        pltpu.VMEM((HALVES, 3, TAPS, part), f32),
        pltpu.VMEM((TOP + rows, part), f32),
        pltpu.VMEM((TOP + rows, part), bf16),
        pltpu.VMEM((TOP + rows, part), bf16),
        pltpu.VMEM((TOP + rows, BLOCK), f32),
        pltpu.VMEM((HALVES, rows, part), f32),
        pltpu.VMEM((HALVES, rows, part), f32),
        kernels, kernels, pltpu.VMEM((HALF, HALVES, BLOCK), f32),
        pltpu.VMEM((HALVES, PAD, 2 * BLOCK), f32),
        blocks, blocks,
        pltpu.VMEM((HALF * GROUP, BLOCK), f32),
        pltpu.VMEM((HALF * GROUP, BLOCK), f32),
        blocks, blocks,
        pltpu.VMEM((rows, part), bf16),
        pltpu.VMEM((rows, part), bf16),
        pltpu.SemaphoreType.REGULAR,
        dma((len(args),)),
        dma((3,)), dma((3,)),
        dma, dma,
        dma((4,)), dma((4,)),
        dma, dma((SIDE,)),
        dma, dma,
        dma((HALVES,)), dma((HALVES,)),
        dma((HALVES,)), dma((HALVES, SIDE)),
        dma, dma((SIDE,)),
    ]
    received = pl.pallas_call(
        tick,
        out_shape=jax.ShapeDtypeStruct((rows, chans), f32),
        in_specs=[anywhere] * len(args),
        out_specs=pl.BlockSpec(memory_space=pltpu.VMEM),
        scratch_shapes=scratch,
        compiler_params=pltpu.CompilerParams(collective_id=0, has_side_effects=True, vmem_limit_bytes=48 << 20),
        name="tick",
    )(*(pltpu.with_memory_space_constraint(arg, pltpu.HBM) for arg in args))
    return received[None]


def solution(mesh):
    in_specs = (
        P("section", "ctx", "tp"),
        P("section", "ctx", "tp"),
        P("section", None, None, "tp"),
        P("section", "tp"),
    )
    out_specs = P("section", "ctx", "tp")
    return jax.shard_map(local, mesh=mesh, in_specs=in_specs, out_specs=out_specs, check_vma=False)
```

```python
import functools

import jax
import jax.numpy as jnp
import numpy as np
from jax import lax
from jax.experimental import pallas as pl
from jax.experimental.pallas import tpu as pltpu
from jax.sharding import PartitionSpec as P

CHAN = 4096
TAPS = 3
BLOCK = 128
SEQ = 8192
HALF = SEQ // BLOCK
SPAN = 2 * HALF
TOTAL = SPAN * BLOCK
ROWS = HALF + 1
PAD = 72
SIDE = 8
TOGETHER = 8
GROUP = 16
HALVES = 2
HALO = 2
TOP = 16
MESH = pl.DeviceIdType.MESH


def unit_pair(position, period):
    mirror = period - position
    folded = np.minimum(position, mirror)
    angle = folded.astype(np.float32) * np.float32(2 * np.pi / period)
    cosine = np.where(4 * folded == period, 0.0, np.cos(angle)).astype(np.float32)
    sine = np.where((folded == 0) | (2 * folded == period), 0.0, np.sin(angle)).astype(np.float32)
    sine = np.where(position > mirror, -sine, sine)
    return cosine, -sine


def padded(rows):
    return np.pad(rows, ((0, PAD - ROWS), (0, 0)))


def tables():
    k1 = np.arange(ROWS)
    a = np.arange(HALF)
    b = np.arange(BLOCK)
    outer_re, outer_im = unit_pair(k1[:, None] * a[None, :] % SPAN, SPAN)
    inner_re, inner_im = unit_pair(b[:, None] * b[None, :] % BLOCK, BLOCK)
    turn_re, turn_im = unit_pair(k1[:, None] * b[None, :] % TOTAL, TOTAL)
    fold = np.full((ROWS, 1), 2.0 / TOTAL, np.float32)
    fold[0] = fold[-1] = 1.0 / TOTAL
    outer = jnp.asarray(np.concatenate([padded(outer_re), padded(outer_im)]), jnp.bfloat16)
    forward = jnp.asarray(np.block([[inner_re, inner_im], [-inner_im, inner_re]]), jnp.bfloat16)
    inverse = jnp.asarray(np.block([[inner_re, -inner_im], [inner_im, inner_re]]), jnp.bfloat16)
    turn = jnp.asarray(np.stack([padded(turn_re), padded(turn_im)]), jnp.float32)
    rounded = [padded(np.asarray(t.astype(jnp.bfloat16)).astype(np.float32) * fold) for t in (outer_re, outer_im)]
    final = jnp.asarray(np.concatenate(rounded).T, jnp.bfloat16)
    return outer, forward, inverse, turn, final


def dot32(left, right):
    return lax.dot_general(left, right, (((1,), (0,)), ((), ())), preferred_element_type=jnp.float32)


def transform(slabs, outer, forward, turn):
    first = dot32(outer[...], jnp.concatenate(slabs, axis=1).astype(jnp.bfloat16))
    turned = []
    for j in range(len(slabs)):
        re = first[:PAD, j * BLOCK : (j + 1) * BLOCK]
        im = first[PAD:, j * BLOCK : (j + 1) * BLOCK]
        turned_re = turn[0] * re - turn[1] * im
        turned_im = turn[0] * im + turn[1] * re
        turned.append(jnp.concatenate([turned_re, turned_im], axis=1).astype(jnp.bfloat16))
    return dot32(jnp.concatenate(turned, axis=0), forward[...])


def untransform(spec, count, filt_re, filt_im, inverse, turn, final):
    weighted = []
    for j in range(count):
        re = spec[j * PAD : (j + 1) * PAD, :BLOCK]
        im = spec[j * PAD : (j + 1) * PAD, BLOCK:]
        out_re = re * filt_re - im * filt_im
        out_im = re * filt_im + im * filt_re
        weighted.append(jnp.concatenate([out_re, out_im], axis=1).astype(jnp.bfloat16))
    back = dot32(jnp.concatenate(weighted, axis=0), inverse[...])
    unturned = []
    for j in range(count):
        re = back[j * PAD : (j + 1) * PAD, :BLOCK]
        im = back[j * PAD : (j + 1) * PAD, BLOCK:]
        out_re = turn[0] * re + turn[1] * im
        out_im = turn[0] * im - turn[1] * re
        unturned.append(jnp.concatenate([out_re, out_im], axis=0).astype(jnp.bfloat16))
    return dot32(final[...], jnp.concatenate(unturned, axis=1))


def tick(
    x_hbm, filter_hbm, short_hbm, skip_hbm, outer_hbm, forward_hbm, inverse_hbm, turn_hbm, final_hbm, out,
    x, kern, short, skip, outer, forward, inverse, turn, final,
    edge, halo, edge_squares, halo_squares, squares, other_squares, root, root_in, short_in, skip_in, kern_early,
    taps, normed, moved, moved_in, shifted_in, query, base, kern_out, kern_in, kern_wide, filt,
    product, got, wide, result, ready, conv, finished, finished_in,
    met, load_sem, edge_send, edge_recv, sq_send, sq_recv, small_send, small_recv, move_send, move_recv,
    kern_send, kern_recv, prod_send, prod_recv, conv_send, conv_recv, hop_send, hop_recv,
):
    rows, chans = x.shape
    part = chans // HALVES
    section, ctx, tp = lax.axis_index("section"), lax.axis_index("ctx"), lax.axis_index("tp")
    n_section = lax.axis_size("section")
    z, y = ctx // SIDE, ctx % SIDE
    following, before = (ctx + 1) % HALF, (ctx + HALF - 1) % HALF
    onward = (section + 1) % n_section
    step_z, step_y = 3 + 2 * tp, 5 - 2 * tp

    pairs = (
        (x_hbm, x), (filter_hbm, kern), (short_hbm, short), (skip_hbm, skip), (outer_hbm, outer),
        (forward_hbm, forward), (inverse_hbm, inverse), (turn_hbm, turn), (final_hbm, final),
    )
    loads = [pltpu.make_async_copy(src, dst, load_sem.at[i]) for i, (src, dst) in enumerate(pairs)]
    for load in loads:
        load.start()

    barrier = pltpu.get_barrier_semaphore()

    def greet(sem, **to):
        pl.semaphore_signal(sem, inc=1, device_id=to, device_id_type=MESH)

    greet(barrier, tp=1 - tp)
    greet(barrier, ctx=before, tp=0)
    greet(barrier, ctx=before, tp=1)
    for k in range(1, SIDE):
        greet(barrier, ctx=(z + k) % SIDE * SIDE + y)
        greet(barrier, ctx=z * SIDE + (y + k) % SIDE)
    greet(barrier, section=(section + n_section - 1) % n_section)

    loads[0].wait()
    edge[...] = x[rows - HALO :, :]
    total = jnp.zeros((rows, BLOCK), jnp.float32)
    for j in range(chans // BLOCK):
        piece = x[:, j * BLOCK : (j + 1) * BLOCK]
        total = total + piece * piece
    squares[...] = total
    edge_squares[...] = total[rows - HALO :]
    pl.semaphore_wait(barrier, 2 * (SIDE - 1) + 4)

    def remote(src, dst, send, recv, **to):
        return pltpu.make_async_remote_copy(
            src_ref=src, dst_ref=dst, send_sem=send, recv_sem=recv, device_id=to, device_id_type=MESH
        )

    edges = [
        remote(edge, halo, edge_send.at[0], edge_recv.at[0], ctx=following),
        remote(edge_squares, halo_squares.at[0], edge_send.at[1], edge_recv.at[1], ctx=following),
        remote(edge_squares, halo_squares.at[1], edge_send.at[2], edge_recv.at[2], ctx=following, tp=1 - tp),
    ]
    for send in edges:
        send.start()
    swap = remote(squares, other_squares, sq_send, sq_recv, tp=1 - tp)
    swap.start()
    for k in range(1, SIDE):
        greet(met, ctx=(z + k) % SIDE * SIDE + y)

    for load in loads[1:]:
        load.wait()
    late = pl.ds(part, part)
    smalls = [
        remote(short.at[:, :, late], short_in, small_send.at[0], small_recv.at[0], section=onward),
        remote(skip.at[:, late], skip_in, small_send.at[1], small_recv.at[1], section=onward),
        remote(kern, kern_early, small_send.at[2], small_recv.at[2], section=onward),
        remote(root, root_in, small_send.at[3], small_recv.at[3], section=onward),
    ]
    for send in smalls[:3]:
        send.start()
    for f in range(3):
        taps[0, f] = short[f, :, :part].astype(jnp.float32)

    swap.wait_recv()
    mean = jnp.sum(squares[...] + other_squares[...], axis=1, keepdims=True) / CHAN + 1e-06
    scale = lax.rsqrt(mean)
    for send in edges:
        send.wait_recv()
    edge_mean = jnp.sum(halo_squares[0] + halo_squares[1], axis=1, keepdims=True) / CHAN + 1e-06
    edge_normed = jnp.where(ctx == 0, 0.0, halo[...] * lax.rsqrt(edge_mean))
    normed[TOP - HALO : TOP, :] = edge_normed[:, :part].astype(jnp.bfloat16).astype(jnp.float32)
    edge_late = jnp.concatenate([jnp.zeros((TOP - HALO, part), jnp.float32), edge_normed[:, part:]], axis=0)
    moved[:TOP, :] = edge_late.astype(jnp.bfloat16)
    for j in range(part // BLOCK):
        lanes = slice(part + j * BLOCK, part + (j + 1) * BLOCK)
        moved[TOP:, j * BLOCK : (j + 1) * BLOCK] = (x[:, lanes] * scale).astype(jnp.bfloat16)

    def move(row):
        lanes = pl.ds(pl.multiple_of(row * BLOCK, BLOCK), BLOCK)
        return remote(moved.at[:, lanes], moved_in.at[:, lanes], move_send, move_recv.at[row], section=onward)

    def lane_row(i):
        return (z + i * step_z) % SIDE

    for j in range(part // BLOCK):
        lanes = slice(j * BLOCK, (j + 1) * BLOCK)
        normed[TOP:, lanes] = (x[:, lanes] * scale).astype(jnp.bfloat16).astype(jnp.float32)
    pl.semaphore_wait(met, SIDE - 1)

    def features(h, lanes, shifted, gain):
        made = []
        for f in range(3):
            running = taps[h, f, pl.ds(0, 1), lanes] * shifted[0]
            for t in range(1, TAPS):
                running = running + taps[h, f, pl.ds(t, 1), lanes] * shifted[t]
            made.append(running)
        ask = made[0].astype(jnp.bfloat16).astype(jnp.float32)
        gated = (made[1] * made[2]).astype(jnp.bfloat16).astype(jnp.float32)
        return ask, gated, ask * (gain * gated)

    def send_products(h, row, gated, first):
        product[h, pl.ds(row * SIDE, SIDE)] = gated.T.astype(jnp.bfloat16).reshape(SIDE, GROUP, BLOCK)

        def send(r, inner):
            to = row * SIDE + (y + r * step_y) % SIDE
            remote(product.at[h, to], got.at[h, ctx], prod_send.at[h], prod_recv.at[h], ctx=to).start()
            return inner

        lax.fori_loop(jnp.where(first, 1, 0), SIDE, send, 0)

    def early_chunk(i, carry):
        row = lane_row(i)
        lanes = pl.ds(pl.multiple_of(row * BLOCK, BLOCK), BLOCK)
        shifted = [normed[pl.ds(TOP - t, rows), lanes] for t in range(TAPS)]
        ask, gated, direct = features(0, lanes, shifted, skip[:, lanes])
        query[0, :, lanes] = ask
        base[0, :, lanes] = x[:, lanes] + direct
        move(row).start()
        send_products(0, row, gated, i == 0)
        return carry

    lax.fori_loop(0, SIDE, early_chunk, 0)
    pltpu.make_async_copy(product.at[0, ctx], got.at[0, ctx], prod_recv.at[0]).start()

    root[...] = jnp.broadcast_to(jnp.sqrt(mean), (rows, BLOCK)).T[:SIDE]
    smalls[3].start()
    smalls[2].wait_recv()
    kern_wide[:, 0, :] = kern[...].astype(jnp.float32).T[:HALF]
    kern_wide[:, 1, :] = kern_early[...].astype(jnp.float32).T[HALF:]
    kern_out[...] = kern_wide[...].astype(jnp.bfloat16)

    def at(dz, dy):
        return (z + dz) % SIDE * SIDE + (y + dy) % SIDE

    def send_kern(k, carry):
        to = at(k // SIDE * step_z, k % SIDE * step_y)
        remote(kern_out.at[to], kern_in.at[ctx], kern_send, kern_recv, ctx=to).start()
        return carry

    lax.fori_loop(1, HALF, send_kern, 0)
    pltpu.make_async_copy(kern_out.at[ctx], kern_in.at[ctx], kern_recv).start()

    for i in (0, 1, 3):
        smalls[i].wait_recv()
    for f in range(3):
        taps[1, f] = short_in[f].astype(jnp.float32)
    spread = jnp.broadcast_to(root_in[0:1, :], (rows, BLOCK)).T

    def wait_in(dst, sem):
        pltpu.make_async_copy(dst, dst, sem).wait()

    def late_chunk(i, carry):
        row = lane_row(i)
        lanes = pl.ds(pl.multiple_of(row * BLOCK, BLOCK), BLOCK)
        wait_in(moved_in.at[:, lanes], move_recv.at[row])
        shifted_in[...] = moved_in[:, lanes].astype(jnp.float32)
        shifted = [shifted_in[TOP - t : TOP - t + rows, :] for t in range(TAPS)]
        ask, gated, direct = features(1, lanes, shifted, skip_in[:, lanes])
        query[1, :, lanes] = ask
        base[1, :, lanes] = shifted[0] * spread + direct
        send_products(1, row, gated, i == 0)
        return carry

    lax.fori_loop(0, SIDE, late_chunk, 0)
    pltpu.make_async_copy(product.at[1, ctx], got.at[1, ctx], prod_recv.at[1]).start()

    wait_in(kern_in, kern_recv)
    kern_wide[...] = kern_in[...].astype(jnp.float32)
    spec = transform([kern_wide[:, h, :] for h in range(HALVES)], outer, forward, turn)
    for h in range(HALVES):
        filt[h] = spec[h * PAD : (h + 1) * PAD]

    for h in range(HALVES):
        wait_in(got.at[h], prod_recv.at[h])
        wide[...] = got[h].astype(jnp.float32).reshape(wide.shape)

        def group(g, carry):
            ids = [g * TOGETHER + j for j in range(TOGETHER)]
            slabs = [wide[pl.ds(c, HALF, stride=GROUP), :] for c in ids]
            spec = transform(slabs, outer, forward, turn)
            gain = filt[h]
            made = untransform(spec, TOGETHER, gain[:, :BLOCK], gain[:, BLOCK:], inverse, turn, final)
            for j, c in enumerate(ids):
                result[pl.ds(c, HALF, stride=GROUP), :] = made[:, j * BLOCK : (j + 1) * BLOCK]
            return carry

        lax.fori_loop(0, GROUP // TOGETHER, group, 0, unroll=True)
        ready[h] = result[...].reshape(HALF, GROUP, BLOCK).astype(jnp.bfloat16)

        def send_back(k, carry):
            to = at(k // SIDE * step_z, k % SIDE * step_y)
            remote(ready.at[h, to], conv.at[h, ctx], conv_send.at[h], conv_recv.at[h, z], ctx=to).start()
            return carry

        lax.fori_loop(1, HALF, send_back, 0)
        pltpu.make_async_copy(ready.at[h, ctx], conv.at[h, ctx], conv_recv.at[h, z]).start()

    def finish(h, row, lanes):
        blocks = pl.ds(row * SIDE, SIDE)
        wait_in(conv.at[h, blocks], conv_recv.at[h, row])
        got_conv = conv[h, blocks].astype(jnp.float32).reshape(BLOCK, BLOCK).T
        return base[h, :, lanes] + query[h, :, lanes] * got_conv

    def back_row(i):
        return (z + i * (SIDE - step_z)) % SIDE

    def finish_early(i, carry):
        row = back_row(i)
        lanes = pl.ds(pl.multiple_of(row * BLOCK, BLOCK), BLOCK)
        finished[:, lanes] = finish(0, row, lanes).astype(jnp.bfloat16)
        remote(finished.at[:, lanes], finished_in.at[:, lanes], hop_send, hop_recv.at[row], section=onward).start()
        return carry

    lax.fori_loop(0, SIDE, finish_early, 0)

    def take_early(i, carry):
        row = back_row(i)
        lanes = pl.ds(pl.multiple_of(row * BLOCK, BLOCK), BLOCK)
        wait_in(finished_in.at[:, lanes], hop_recv.at[row])
        out[:, lanes] = finished_in[:, lanes].astype(jnp.float32)
        return carry

    def finish_late(i, carry):
        row = back_row(i)
        lanes = pl.ds(pl.multiple_of(row * BLOCK, BLOCK), BLOCK)
        after = pl.ds(pl.multiple_of(part + row * BLOCK, BLOCK), BLOCK)
        out[:, after] = finish(1, row, lanes)
        return carry

    lax.fori_loop(0, SIDE, take_early, 0)
    lax.fori_loop(0, SIDE, finish_late, 0)

    sent = pl.ds(0, HALF - 1)
    for send in (swap, *edges, *smalls):
        send.wait_send()
    wait_in(moved, move_send)
    wait_in(kern_out.at[sent], kern_send)
    for h in range(HALVES):
        wait_in(product.at[h, sent], prod_send.at[h])
        wait_in(ready.at[h, sent], conv_send.at[h])
    wait_in(finished, hop_send)


def local(section_input, long_filter, short_filter, skip_gain):
    rows, chans = section_input.shape[1:]
    part = chans // HALVES
    args = (section_input[0], long_filter[0], short_filter[0], skip_gain, *tables())
    anywhere = pl.BlockSpec(memory_space=pl.ANY)
    f32, bf16 = jnp.float32, jnp.bfloat16
    dma = pltpu.SemaphoreType.DMA
    blocks = pltpu.VMEM((HALVES, HALF, GROUP, BLOCK), bf16)
    kernels = pltpu.VMEM((HALF, HALVES, BLOCK), bf16)
    scratch = [pltpu.VMEM(arg.shape, arg.dtype) for arg in args] + [
        pltpu.VMEM((HALO, chans), f32),
        pltpu.VMEM((HALO, chans), f32),
        pltpu.VMEM((HALO, BLOCK), f32),
        pltpu.VMEM((2, HALO, BLOCK), f32),
        pltpu.VMEM((rows, BLOCK), f32),
        pltpu.VMEM((rows, BLOCK), f32),
        pltpu.VMEM((SIDE, BLOCK), f32),
        pltpu.VMEM((SIDE, BLOCK), f32),
        pltpu.VMEM((3, TAPS, part), bf16),
        pltpu.VMEM((1, part), f32),
        pltpu.VMEM(args[1].shape, bf16),
        pltpu.VMEM((HALVES, 3, TAPS, part), f32),
        pltpu.VMEM((TOP + rows, part), f32),
        pltpu.VMEM((TOP + rows, part), bf16),
        pltpu.VMEM((TOP + rows, part), bf16),
        pltpu.VMEM((TOP + rows, BLOCK), f32),
        pltpu.VMEM((HALVES, rows, part), f32),
        pltpu.VMEM((HALVES, rows, part), f32),
        kernels, kernels, pltpu.VMEM((HALF, HALVES, BLOCK), f32),
        pltpu.VMEM((HALVES, PAD, 2 * BLOCK), f32),
        blocks, blocks,
        pltpu.VMEM((HALF * GROUP, BLOCK), f32),
        pltpu.VMEM((HALF * GROUP, BLOCK), f32),
        blocks, blocks,
        pltpu.VMEM((rows, part), bf16),
        pltpu.VMEM((rows, part), bf16),
        pltpu.SemaphoreType.REGULAR,
        dma((len(args),)),
        dma((3,)), dma((3,)),
        dma, dma,
        dma((4,)), dma((4,)),
        dma, dma((SIDE,)),
        dma, dma,
        dma((HALVES,)), dma((HALVES,)),
        dma((HALVES,)), dma((HALVES, SIDE)),
        dma, dma((SIDE,)),
    ]
    received = pl.pallas_call(
        tick,
        out_shape=jax.ShapeDtypeStruct((rows, chans), f32),
        in_specs=[anywhere] * len(args),
        out_specs=pl.BlockSpec(memory_space=pltpu.VMEM),
        scratch_shapes=scratch,
        compiler_params=pltpu.CompilerParams(collective_id=0, has_side_effects=True, vmem_limit_bytes=48 << 20),
        name="tick",
    )(*(pltpu.with_memory_space_constraint(arg, pltpu.HBM) for arg in args))
    return received[None]


def solution(mesh):
    in_specs = (
        P("section", "ctx", "tp"),
        P("section", "ctx", "tp"),
        P("section", None, None, "tp"),
        P("section", "tp"),
    )
    out_specs = P("section", "ctx", "tp")
    return jax.shard_map(local, mesh=mesh, in_specs=in_specs, out_specs=out_specs, check_vma=False)
```

```python
import functools

import jax
import jax.numpy as jnp
import numpy as np
from jax import lax
from jax.experimental import pallas as pl
from jax.experimental.pallas import tpu as pltpu
from jax.sharding import PartitionSpec as P

CHAN = 4096
TAPS = 3
BLOCK = 128
SEQ = 8192
HALF = SEQ // BLOCK
SPAN = 2 * HALF
TOTAL = SPAN * BLOCK
ROWS = HALF + 1
PAD = 72
SIDE = 8
TOGETHER = 8
GROUP = 16
HALVES = 2
HALO = 2
TOP = 16
MESH = pl.DeviceIdType.MESH


def unit_pair(position, period):
    mirror = period - position
    folded = np.minimum(position, mirror)
    angle = folded.astype(np.float32) * np.float32(2 * np.pi / period)
    cosine = np.where(4 * folded == period, 0.0, np.cos(angle)).astype(np.float32)
    sine = np.where((folded == 0) | (2 * folded == period), 0.0, np.sin(angle)).astype(np.float32)
    sine = np.where(position > mirror, -sine, sine)
    return cosine, -sine


def padded(rows):
    return np.pad(rows, ((0, PAD - ROWS), (0, 0)))


def tables():
    k1 = np.arange(ROWS)
    a = np.arange(HALF)
    b = np.arange(BLOCK)
    outer_re, outer_im = unit_pair(k1[:, None] * a[None, :] % SPAN, SPAN)
    inner_re, inner_im = unit_pair(b[:, None] * b[None, :] % BLOCK, BLOCK)
    turn_re, turn_im = unit_pair(k1[:, None] * b[None, :] % TOTAL, TOTAL)
    fold = np.full((ROWS, 1), 2.0 / TOTAL, np.float32)
    fold[0] = fold[-1] = 1.0 / TOTAL
    outer = jnp.asarray(np.concatenate([padded(outer_re), padded(outer_im)]), jnp.bfloat16)
    forward = jnp.asarray(np.block([[inner_re, inner_im], [-inner_im, inner_re]]), jnp.bfloat16)
    inverse = jnp.asarray(np.block([[inner_re, -inner_im], [inner_im, inner_re]]), jnp.bfloat16)
    turn = jnp.asarray(np.stack([padded(turn_re), padded(turn_im)]), jnp.float32)
    rounded = [padded(np.asarray(t.astype(jnp.bfloat16)).astype(np.float32) * fold) for t in (outer_re, outer_im)]
    final = jnp.asarray(np.concatenate(rounded).T, jnp.bfloat16)
    return outer, forward, inverse, turn, final


def dot32(left, right):
    return lax.dot_general(left, right, (((1,), (0,)), ((), ())), preferred_element_type=jnp.float32)


def transform(slabs, outer, forward, turn):
    first = dot32(outer[...], jnp.concatenate(slabs, axis=1).astype(jnp.bfloat16))
    turned = []
    for j in range(len(slabs)):
        re = first[:PAD, j * BLOCK : (j + 1) * BLOCK]
        im = first[PAD:, j * BLOCK : (j + 1) * BLOCK]
        turned_re = turn[0] * re - turn[1] * im
        turned_im = turn[0] * im + turn[1] * re
        turned.append(jnp.concatenate([turned_re, turned_im], axis=1).astype(jnp.bfloat16))
    return dot32(jnp.concatenate(turned, axis=0), forward[...])


def untransform(spec, count, filt_re, filt_im, inverse, turn, final):
    weighted = []
    for j in range(count):
        re = spec[j * PAD : (j + 1) * PAD, :BLOCK]
        im = spec[j * PAD : (j + 1) * PAD, BLOCK:]
        out_re = re * filt_re - im * filt_im
        out_im = re * filt_im + im * filt_re
        weighted.append(jnp.concatenate([out_re, out_im], axis=1).astype(jnp.bfloat16))
    back = dot32(jnp.concatenate(weighted, axis=0), inverse[...])
    unturned = []
    for j in range(count):
        re = back[j * PAD : (j + 1) * PAD, :BLOCK]
        im = back[j * PAD : (j + 1) * PAD, BLOCK:]
        out_re = turn[0] * re + turn[1] * im
        out_im = turn[0] * im - turn[1] * re
        unturned.append(jnp.concatenate([out_re, out_im], axis=0).astype(jnp.bfloat16))
    return dot32(final[...], jnp.concatenate(unturned, axis=1))


def tick(
    x_hbm, filter_hbm, short_hbm, skip_hbm, outer_hbm, forward_hbm, inverse_hbm, turn_hbm, final_hbm, out,
    x, kern, short, skip, outer, forward, inverse, turn, final,
    edge, halo, edge_squares, halo_squares, squares, other_squares, root, root_in, short_in, skip_in, kern_early,
    taps, normed, moved, moved_in, shifted_in, query, base, kern_out, kern_in, kern_wide, filt,
    product, got, wide, result, ready, conv, finished, finished_in,
    met, load_sem, edge_send, edge_recv, sq_send, sq_recv, small_send, small_recv, move_send, move_recv,
    kern_send, kern_recv, prod_send, prod_recv, conv_send, conv_recv, hop_send, hop_recv,
):
    rows, chans = x.shape
    part = chans // HALVES
    section, ctx, tp = lax.axis_index("section"), lax.axis_index("ctx"), lax.axis_index("tp")
    n_section = lax.axis_size("section")
    z, y = ctx // SIDE, ctx % SIDE
    following, before = (ctx + 1) % HALF, (ctx + HALF - 1) % HALF
    onward = (section + 1) % n_section
    step_z, step_y = 7 - 6 * tp, 3 + 2 * tp

    pairs = (
        (x_hbm, x), (filter_hbm, kern), (short_hbm, short), (skip_hbm, skip), (outer_hbm, outer),
        (forward_hbm, forward), (inverse_hbm, inverse), (turn_hbm, turn), (final_hbm, final),
    )
    loads = [pltpu.make_async_copy(src, dst, load_sem.at[i]) for i, (src, dst) in enumerate(pairs)]
    for load in loads:
        load.start()

    barrier = pltpu.get_barrier_semaphore()

    def greet(sem, **to):
        pl.semaphore_signal(sem, inc=1, device_id=to, device_id_type=MESH)

    greet(barrier, tp=1 - tp)
    greet(barrier, ctx=before, tp=0)
    greet(barrier, ctx=before, tp=1)
    for k in range(1, SIDE):
        greet(barrier, ctx=(z + k) % SIDE * SIDE + y)
        greet(barrier, ctx=z * SIDE + (y + k) % SIDE)
    greet(barrier, section=(section + n_section - 1) % n_section)

    loads[0].wait()
    edge[...] = x[rows - HALO :, :]
    total = jnp.zeros((rows, BLOCK), jnp.float32)
    for j in range(chans // BLOCK):
        piece = x[:, j * BLOCK : (j + 1) * BLOCK]
        total = total + piece * piece
    squares[...] = total
    edge_squares[...] = total[rows - HALO :]
    pl.semaphore_wait(barrier, 2 * (SIDE - 1) + 4)

    def remote(src, dst, send, recv, **to):
        return pltpu.make_async_remote_copy(
            src_ref=src, dst_ref=dst, send_sem=send, recv_sem=recv, device_id=to, device_id_type=MESH
        )

    edges = [
        remote(edge, halo, edge_send.at[0], edge_recv.at[0], ctx=following),
        remote(edge_squares, halo_squares.at[0], edge_send.at[1], edge_recv.at[1], ctx=following),
        remote(edge_squares, halo_squares.at[1], edge_send.at[2], edge_recv.at[2], ctx=following, tp=1 - tp),
    ]
    for send in edges:
        send.start()
    swap = remote(squares, other_squares, sq_send, sq_recv, tp=1 - tp)
    swap.start()
    for k in range(1, SIDE):
        greet(met, ctx=(z + k) % SIDE * SIDE + y)

    for load in loads[1:]:
        load.wait()
    late = pl.ds(part, part)
    smalls = [
        remote(short.at[:, :, late], short_in, small_send.at[0], small_recv.at[0], section=onward),
        remote(skip.at[:, late], skip_in, small_send.at[1], small_recv.at[1], section=onward),
        remote(kern, kern_early, small_send.at[2], small_recv.at[2], section=onward),
        remote(root, root_in, small_send.at[3], small_recv.at[3], section=onward),
    ]
    for send in smalls[:3]:
        send.start()
    for f in range(3):
        taps[0, f] = short[f, :, :part].astype(jnp.float32)

    swap.wait_recv()
    mean = jnp.sum(squares[...] + other_squares[...], axis=1, keepdims=True) / CHAN + 1e-06
    scale = lax.rsqrt(mean)
    for send in edges:
        send.wait_recv()
    edge_mean = jnp.sum(halo_squares[0] + halo_squares[1], axis=1, keepdims=True) / CHAN + 1e-06
    edge_normed = jnp.where(ctx == 0, 0.0, halo[...] * lax.rsqrt(edge_mean))
    normed[TOP - HALO : TOP, :] = edge_normed[:, :part].astype(jnp.bfloat16).astype(jnp.float32)
    edge_late = jnp.concatenate([jnp.zeros((TOP - HALO, part), jnp.float32), edge_normed[:, part:]], axis=0)
    moved[:TOP, :] = edge_late.astype(jnp.bfloat16)
    for j in range(part // BLOCK):
        lanes = slice(part + j * BLOCK, part + (j + 1) * BLOCK)
        moved[TOP:, j * BLOCK : (j + 1) * BLOCK] = (x[:, lanes] * scale).astype(jnp.bfloat16)

    def move(row):
        lanes = pl.ds(pl.multiple_of(row * BLOCK, BLOCK), BLOCK)
        return remote(moved.at[:, lanes], moved_in.at[:, lanes], move_send, move_recv.at[row], section=onward)

    def lane_row(i):
        return (z + i * step_z) % SIDE

    for j in range(part // BLOCK):
        lanes = slice(j * BLOCK, (j + 1) * BLOCK)
        normed[TOP:, lanes] = (x[:, lanes] * scale).astype(jnp.bfloat16).astype(jnp.float32)
    pl.semaphore_wait(met, SIDE - 1)

    def features(h, lanes, shifted, gain):
        made = []
        for f in range(3):
            running = taps[h, f, pl.ds(0, 1), lanes] * shifted[0]
            for t in range(1, TAPS):
                running = running + taps[h, f, pl.ds(t, 1), lanes] * shifted[t]
            made.append(running)
        ask = made[0].astype(jnp.bfloat16).astype(jnp.float32)
        gated = (made[1] * made[2]).astype(jnp.bfloat16).astype(jnp.float32)
        return ask, gated, ask * (gain * gated)

    def send_products(h, row, gated, first):
        product[h, pl.ds(row * SIDE, SIDE)] = gated.T.astype(jnp.bfloat16).reshape(SIDE, GROUP, BLOCK)

        def send(r, inner):
            to = row * SIDE + (y + r * step_y) % SIDE
            remote(product.at[h, to], got.at[h, ctx], prod_send.at[h], prod_recv.at[h], ctx=to).start()
            return inner

        lax.fori_loop(jnp.where(first, 1, 0), SIDE, send, 0)

    def early_chunk(i, carry):
        row = lane_row(i)
        lanes = pl.ds(pl.multiple_of(row * BLOCK, BLOCK), BLOCK)
        shifted = [normed[pl.ds(TOP - t, rows), lanes] for t in range(TAPS)]
        ask, gated, direct = features(0, lanes, shifted, skip[:, lanes])
        query[0, :, lanes] = ask
        base[0, :, lanes] = x[:, lanes] + direct
        move(row).start()
        send_products(0, row, gated, i == 0)
        return carry

    lax.fori_loop(0, SIDE, early_chunk, 0)
    pltpu.make_async_copy(product.at[0, ctx], got.at[0, ctx], prod_recv.at[0]).start()

    root[...] = jnp.broadcast_to(jnp.sqrt(mean), (rows, BLOCK)).T[:SIDE]
    smalls[3].start()
    smalls[2].wait_recv()
    kern_wide[:, 0, :] = kern[...].astype(jnp.float32).T[:HALF]
    kern_wide[:, 1, :] = kern_early[...].astype(jnp.float32).T[HALF:]
    kern_out[...] = kern_wide[...].astype(jnp.bfloat16)

    def at(dz, dy):
        return (z + dz) % SIDE * SIDE + (y + dy) % SIDE

    def send_kern(k, carry):
        to = at(k // SIDE * step_z, k % SIDE * step_y)
        remote(kern_out.at[to], kern_in.at[ctx], kern_send, kern_recv, ctx=to).start()
        return carry

    lax.fori_loop(1, HALF, send_kern, 0)
    pltpu.make_async_copy(kern_out.at[ctx], kern_in.at[ctx], kern_recv).start()

    for i in (0, 1, 3):
        smalls[i].wait_recv()
    for f in range(3):
        taps[1, f] = short_in[f].astype(jnp.float32)
    spread = jnp.broadcast_to(root_in[0:1, :], (rows, BLOCK)).T

    def wait_in(dst, sem):
        pltpu.make_async_copy(dst, dst, sem).wait()

    def late_chunk(i, carry):
        row = lane_row(i)
        lanes = pl.ds(pl.multiple_of(row * BLOCK, BLOCK), BLOCK)
        wait_in(moved_in.at[:, lanes], move_recv.at[row])
        shifted_in[...] = moved_in[:, lanes].astype(jnp.float32)
        shifted = [shifted_in[TOP - t : TOP - t + rows, :] for t in range(TAPS)]
        ask, gated, direct = features(1, lanes, shifted, skip_in[:, lanes])
        query[1, :, lanes] = ask
        base[1, :, lanes] = shifted[0] * spread + direct
        send_products(1, row, gated, i == 0)
        return carry

    lax.fori_loop(0, SIDE, late_chunk, 0)
    pltpu.make_async_copy(product.at[1, ctx], got.at[1, ctx], prod_recv.at[1]).start()

    wait_in(kern_in, kern_recv)
    kern_wide[...] = kern_in[...].astype(jnp.float32)
    spec = transform([kern_wide[:, h, :] for h in range(HALVES)], outer, forward, turn)
    for h in range(HALVES):
        filt[h] = spec[h * PAD : (h + 1) * PAD]

    for h in range(HALVES):
        wait_in(got.at[h], prod_recv.at[h])
        wide[...] = got[h].astype(jnp.float32).reshape(wide.shape)

        def group(g, carry):
            ids = [g * TOGETHER + j for j in range(TOGETHER)]
            slabs = [wide[pl.ds(c, HALF, stride=GROUP), :] for c in ids]
            spec = transform(slabs, outer, forward, turn)
            gain = filt[h]
            made = untransform(spec, TOGETHER, gain[:, :BLOCK], gain[:, BLOCK:], inverse, turn, final)
            for j, c in enumerate(ids):
                result[pl.ds(c, HALF, stride=GROUP), :] = made[:, j * BLOCK : (j + 1) * BLOCK]
            return carry

        lax.fori_loop(0, GROUP // TOGETHER, group, 0, unroll=True)
        ready[h] = result[...].reshape(HALF, GROUP, BLOCK).astype(jnp.bfloat16)

        def send_back(k, carry):
            to = at(k // SIDE * step_z, k % SIDE * step_y)
            remote(ready.at[h, to], conv.at[h, ctx], conv_send.at[h], conv_recv.at[h, z], ctx=to).start()
            return carry

        lax.fori_loop(1, HALF, send_back, 0)
        pltpu.make_async_copy(ready.at[h, ctx], conv.at[h, ctx], conv_recv.at[h, z]).start()

    def finish(h, row, lanes):
        blocks = pl.ds(row * SIDE, SIDE)
        wait_in(conv.at[h, blocks], conv_recv.at[h, row])
        got_conv = conv[h, blocks].astype(jnp.float32).reshape(BLOCK, BLOCK).T
        return base[h, :, lanes] + query[h, :, lanes] * got_conv

    def back_row(i):
        return (z + i * (SIDE - step_z)) % SIDE

    def finish_early(i, carry):
        row = back_row(i)
        lanes = pl.ds(pl.multiple_of(row * BLOCK, BLOCK), BLOCK)
        finished[:, lanes] = finish(0, row, lanes).astype(jnp.bfloat16)
        remote(finished.at[:, lanes], finished_in.at[:, lanes], hop_send, hop_recv.at[row], section=onward).start()
        return carry

    lax.fori_loop(0, SIDE, finish_early, 0)

    def take_early(i, carry):
        row = back_row(i)
        lanes = pl.ds(pl.multiple_of(row * BLOCK, BLOCK), BLOCK)
        wait_in(finished_in.at[:, lanes], hop_recv.at[row])
        out[:, lanes] = finished_in[:, lanes].astype(jnp.float32)
        return carry

    def finish_late(i, carry):
        row = back_row(i)
        lanes = pl.ds(pl.multiple_of(row * BLOCK, BLOCK), BLOCK)
        after = pl.ds(pl.multiple_of(part + row * BLOCK, BLOCK), BLOCK)
        out[:, after] = finish(1, row, lanes)
        return carry

    lax.fori_loop(0, SIDE, take_early, 0)
    lax.fori_loop(0, SIDE, finish_late, 0)

    sent = pl.ds(0, HALF - 1)
    for send in (swap, *edges, *smalls):
        send.wait_send()
    wait_in(moved, move_send)
    wait_in(kern_out.at[sent], kern_send)
    for h in range(HALVES):
        wait_in(product.at[h, sent], prod_send.at[h])
        wait_in(ready.at[h, sent], conv_send.at[h])
    wait_in(finished, hop_send)


def local(section_input, long_filter, short_filter, skip_gain):
    rows, chans = section_input.shape[1:]
    part = chans // HALVES
    args = (section_input[0], long_filter[0], short_filter[0], skip_gain, *tables())
    anywhere = pl.BlockSpec(memory_space=pl.ANY)
    f32, bf16 = jnp.float32, jnp.bfloat16
    dma = pltpu.SemaphoreType.DMA
    blocks = pltpu.VMEM((HALVES, HALF, GROUP, BLOCK), bf16)
    kernels = pltpu.VMEM((HALF, HALVES, BLOCK), bf16)
    scratch = [pltpu.VMEM(arg.shape, arg.dtype) for arg in args] + [
        pltpu.VMEM((HALO, chans), f32),
        pltpu.VMEM((HALO, chans), f32),
        pltpu.VMEM((HALO, BLOCK), f32),
        pltpu.VMEM((2, HALO, BLOCK), f32),
        pltpu.VMEM((rows, BLOCK), f32),
        pltpu.VMEM((rows, BLOCK), f32),
        pltpu.VMEM((SIDE, BLOCK), f32),
        pltpu.VMEM((SIDE, BLOCK), f32),
        pltpu.VMEM((3, TAPS, part), bf16),
        pltpu.VMEM((1, part), f32),
        pltpu.VMEM(args[1].shape, bf16),
        pltpu.VMEM((HALVES, 3, TAPS, part), f32),
        pltpu.VMEM((TOP + rows, part), f32),
        pltpu.VMEM((TOP + rows, part), bf16),
        pltpu.VMEM((TOP + rows, part), bf16),
        pltpu.VMEM((TOP + rows, BLOCK), f32),
        pltpu.VMEM((HALVES, rows, part), f32),
        pltpu.VMEM((HALVES, rows, part), f32),
        kernels, kernels, pltpu.VMEM((HALF, HALVES, BLOCK), f32),
        pltpu.VMEM((HALVES, PAD, 2 * BLOCK), f32),
        blocks, blocks,
        pltpu.VMEM((HALF * GROUP, BLOCK), f32),
        pltpu.VMEM((HALF * GROUP, BLOCK), f32),
        blocks, blocks,
        pltpu.VMEM((rows, part), bf16),
        pltpu.VMEM((rows, part), bf16),
        pltpu.SemaphoreType.REGULAR,
        dma((len(args),)),
        dma((3,)), dma((3,)),
        dma, dma,
        dma((4,)), dma((4,)),
        dma, dma((SIDE,)),
        dma, dma,
        dma((HALVES,)), dma((HALVES,)),
        dma((HALVES,)), dma((HALVES, SIDE)),
        dma, dma((SIDE,)),
    ]
    received = pl.pallas_call(
        tick,
        out_shape=jax.ShapeDtypeStruct((rows, chans), f32),
        in_specs=[anywhere] * len(args),
        out_specs=pl.BlockSpec(memory_space=pltpu.VMEM),
        scratch_shapes=scratch,
        compiler_params=pltpu.CompilerParams(collective_id=0, has_side_effects=True, vmem_limit_bytes=48 << 20),
        name="tick",
    )(*(pltpu.with_memory_space_constraint(arg, pltpu.HBM) for arg in args))
    return received[None]


def solution(mesh):
    in_specs = (
        P("section", "ctx", "tp"),
        P("section", "ctx", "tp"),
        P("section", None, None, "tp"),
        P("section", "tp"),
    )
    out_specs = P("section", "ctx", "tp")
    return jax.shard_map(local, mesh=mesh, in_specs=in_specs, out_specs=out_specs, check_vma=False)
```

```python
import functools

import jax
import jax.numpy as jnp
import numpy as np
from jax import lax
from jax.experimental import pallas as pl
from jax.experimental.pallas import tpu as pltpu
from jax.sharding import PartitionSpec as P

CHAN = 4096
TAPS = 3
BLOCK = 128
SEQ = 8192
HALF = SEQ // BLOCK
SPAN = 2 * HALF
TOTAL = SPAN * BLOCK
ROWS = HALF + 1
PAD = 72
SIDE = 8
TOGETHER = 8
GROUP = 16
HALVES = 2
HALO = 2
TOP = 16
MESH = pl.DeviceIdType.MESH


def unit_pair(position, period):
    mirror = period - position
    folded = np.minimum(position, mirror)
    angle = folded.astype(np.float32) * np.float32(2 * np.pi / period)
    cosine = np.where(4 * folded == period, 0.0, np.cos(angle)).astype(np.float32)
    sine = np.where((folded == 0) | (2 * folded == period), 0.0, np.sin(angle)).astype(np.float32)
    sine = np.where(position > mirror, -sine, sine)
    return cosine, -sine


def padded(rows):
    return np.pad(rows, ((0, PAD - ROWS), (0, 0)))


def tables():
    k1 = np.arange(ROWS)
    a = np.arange(HALF)
    b = np.arange(BLOCK)
    outer_re, outer_im = unit_pair(k1[:, None] * a[None, :] % SPAN, SPAN)
    inner_re, inner_im = unit_pair(b[:, None] * b[None, :] % BLOCK, BLOCK)
    turn_re, turn_im = unit_pair(k1[:, None] * b[None, :] % TOTAL, TOTAL)
    fold = np.full((ROWS, 1), 2.0 / TOTAL, np.float32)
    fold[0] = fold[-1] = 1.0 / TOTAL
    outer = jnp.asarray(np.concatenate([padded(outer_re), padded(outer_im)]), jnp.bfloat16)
    forward = jnp.asarray(np.block([[inner_re, inner_im], [-inner_im, inner_re]]), jnp.bfloat16)
    inverse = jnp.asarray(np.block([[inner_re, -inner_im], [inner_im, inner_re]]), jnp.bfloat16)
    turn = jnp.asarray(np.stack([padded(turn_re), padded(turn_im)]), jnp.float32)
    rounded = [padded(np.asarray(t.astype(jnp.bfloat16)).astype(np.float32) * fold) for t in (outer_re, outer_im)]
    final = jnp.asarray(np.concatenate(rounded).T, jnp.bfloat16)
    return outer, forward, inverse, turn, final


def dot32(left, right):
    return lax.dot_general(left, right, (((1,), (0,)), ((), ())), preferred_element_type=jnp.float32)


def transform(slabs, outer, forward, turn):
    first = dot32(outer[...], jnp.concatenate(slabs, axis=1).astype(jnp.bfloat16))
    turned = []
    for j in range(len(slabs)):
        re = first[:PAD, j * BLOCK : (j + 1) * BLOCK]
        im = first[PAD:, j * BLOCK : (j + 1) * BLOCK]
        turned_re = turn[0] * re - turn[1] * im
        turned_im = turn[0] * im + turn[1] * re
        turned.append(jnp.concatenate([turned_re, turned_im], axis=1).astype(jnp.bfloat16))
    return dot32(jnp.concatenate(turned, axis=0), forward[...])


def untransform(spec, count, filt_re, filt_im, inverse, turn, final):
    weighted = []
    for j in range(count):
        re = spec[j * PAD : (j + 1) * PAD, :BLOCK]
        im = spec[j * PAD : (j + 1) * PAD, BLOCK:]
        out_re = re * filt_re - im * filt_im
        out_im = re * filt_im + im * filt_re
        weighted.append(jnp.concatenate([out_re, out_im], axis=1).astype(jnp.bfloat16))
    back = dot32(jnp.concatenate(weighted, axis=0), inverse[...])
    unturned = []
    for j in range(count):
        re = back[j * PAD : (j + 1) * PAD, :BLOCK]
        im = back[j * PAD : (j + 1) * PAD, BLOCK:]
        out_re = turn[0] * re + turn[1] * im
        out_im = turn[0] * im - turn[1] * re
        unturned.append(jnp.concatenate([out_re, out_im], axis=0).astype(jnp.bfloat16))
    return dot32(final[...], jnp.concatenate(unturned, axis=1))


def tick(
    x_hbm, filter_hbm, short_hbm, skip_hbm, outer_hbm, forward_hbm, inverse_hbm, turn_hbm, final_hbm, out,
    x, kern, short, skip, outer, forward, inverse, turn, final,
    edge, halo, edge_squares, halo_squares, squares, other_squares, root, root_in, short_in, skip_in, kern_early,
    taps, normed, moved, moved_in, shifted_in, query, base, kern_out, kern_in, kern_wide, filt,
    product, got, wide, result, ready, conv, finished, finished_in,
    met, load_sem, edge_send, edge_recv, sq_send, sq_recv, small_send, small_recv, move_send, move_recv,
    kern_send, kern_recv, prod_send, prod_recv, conv_send, conv_recv, hop_send, hop_recv,
):
    rows, chans = x.shape
    part = chans // HALVES
    section, ctx, tp = lax.axis_index("section"), lax.axis_index("ctx"), lax.axis_index("tp")
    n_section = lax.axis_size("section")
    z, y = ctx // SIDE, ctx % SIDE
    following, before = (ctx + 1) % HALF, (ctx + HALF - 1) % HALF
    onward = (section + 1) % n_section
    step_z, step_y = 7 - 6 * tp, 7 - 6 * tp

    pairs = (
        (x_hbm, x), (filter_hbm, kern), (short_hbm, short), (skip_hbm, skip), (outer_hbm, outer),
        (forward_hbm, forward), (inverse_hbm, inverse), (turn_hbm, turn), (final_hbm, final),
    )
    loads = [pltpu.make_async_copy(src, dst, load_sem.at[i]) for i, (src, dst) in enumerate(pairs)]
    for load in loads:
        load.start()

    barrier = pltpu.get_barrier_semaphore()

    def greet(sem, **to):
        pl.semaphore_signal(sem, inc=1, device_id=to, device_id_type=MESH)

    greet(barrier, tp=1 - tp)
    greet(barrier, ctx=before, tp=0)
    greet(barrier, ctx=before, tp=1)
    for k in range(1, SIDE):
        greet(barrier, ctx=(z + k) % SIDE * SIDE + y)
        greet(barrier, ctx=z * SIDE + (y + k) % SIDE)
    greet(barrier, section=(section + n_section - 1) % n_section)

    loads[0].wait()
    edge[...] = x[rows - HALO :, :]
    total = jnp.zeros((rows, BLOCK), jnp.float32)
    for j in range(chans // BLOCK):
        piece = x[:, j * BLOCK : (j + 1) * BLOCK]
        total = total + piece * piece
    squares[...] = total
    edge_squares[...] = total[rows - HALO :]
    pl.semaphore_wait(barrier, 2 * (SIDE - 1) + 4)

    def remote(src, dst, send, recv, **to):
        return pltpu.make_async_remote_copy(
            src_ref=src, dst_ref=dst, send_sem=send, recv_sem=recv, device_id=to, device_id_type=MESH
        )

    edges = [
        remote(edge, halo, edge_send.at[0], edge_recv.at[0], ctx=following),
        remote(edge_squares, halo_squares.at[0], edge_send.at[1], edge_recv.at[1], ctx=following),
        remote(edge_squares, halo_squares.at[1], edge_send.at[2], edge_recv.at[2], ctx=following, tp=1 - tp),
    ]
    for send in edges:
        send.start()
    swap = remote(squares, other_squares, sq_send, sq_recv, tp=1 - tp)
    swap.start()
    for k in range(1, SIDE):
        greet(met, ctx=(z + k) % SIDE * SIDE + y)

    for load in loads[1:]:
        load.wait()
    late = pl.ds(part, part)
    smalls = [
        remote(short.at[:, :, late], short_in, small_send.at[0], small_recv.at[0], section=onward),
        remote(skip.at[:, late], skip_in, small_send.at[1], small_recv.at[1], section=onward),
        remote(kern, kern_early, small_send.at[2], small_recv.at[2], section=onward),
        remote(root, root_in, small_send.at[3], small_recv.at[3], section=onward),
    ]
    for send in smalls[:3]:
        send.start()
    for f in range(3):
        taps[0, f] = short[f, :, :part].astype(jnp.float32)

    swap.wait_recv()
    mean = jnp.sum(squares[...] + other_squares[...], axis=1, keepdims=True) / CHAN + 1e-06
    scale = lax.rsqrt(mean)
    for send in edges:
        send.wait_recv()
    edge_mean = jnp.sum(halo_squares[0] + halo_squares[1], axis=1, keepdims=True) / CHAN + 1e-06
    edge_normed = jnp.where(ctx == 0, 0.0, halo[...] * lax.rsqrt(edge_mean))
    normed[TOP - HALO : TOP, :] = edge_normed[:, :part].astype(jnp.bfloat16).astype(jnp.float32)
    edge_late = jnp.concatenate([jnp.zeros((TOP - HALO, part), jnp.float32), edge_normed[:, part:]], axis=0)
    moved[:TOP, :] = edge_late.astype(jnp.bfloat16)
    for j in range(part // BLOCK):
        lanes = slice(part + j * BLOCK, part + (j + 1) * BLOCK)
        moved[TOP:, j * BLOCK : (j + 1) * BLOCK] = (x[:, lanes] * scale).astype(jnp.bfloat16)

    def move(row):
        lanes = pl.ds(pl.multiple_of(row * BLOCK, BLOCK), BLOCK)
        return remote(moved.at[:, lanes], moved_in.at[:, lanes], move_send, move_recv.at[row], section=onward)

    def lane_row(i):
        return (z + i * step_z) % SIDE

    for j in range(part // BLOCK):
        lanes = slice(j * BLOCK, (j + 1) * BLOCK)
        normed[TOP:, lanes] = (x[:, lanes] * scale).astype(jnp.bfloat16).astype(jnp.float32)
    pl.semaphore_wait(met, SIDE - 1)

    def features(h, lanes, shifted, gain):
        made = []
        for f in range(3):
            running = taps[h, f, pl.ds(0, 1), lanes] * shifted[0]
            for t in range(1, TAPS):
                running = running + taps[h, f, pl.ds(t, 1), lanes] * shifted[t]
            made.append(running)
        ask = made[0].astype(jnp.bfloat16).astype(jnp.float32)
        gated = (made[1] * made[2]).astype(jnp.bfloat16).astype(jnp.float32)
        return ask, gated, ask * (gain * gated)

    def send_products(h, row, gated, first):
        product[h, pl.ds(row * SIDE, SIDE)] = gated.T.astype(jnp.bfloat16).reshape(SIDE, GROUP, BLOCK)

        def send(r, inner):
            to = row * SIDE + (y + r * step_y) % SIDE
            remote(product.at[h, to], got.at[h, ctx], prod_send.at[h], prod_recv.at[h], ctx=to).start()
            return inner

        lax.fori_loop(jnp.where(first, 1, 0), SIDE, send, 0)

    def early_chunk(i, carry):
        row = lane_row(i)
        lanes = pl.ds(pl.multiple_of(row * BLOCK, BLOCK), BLOCK)
        shifted = [normed[pl.ds(TOP - t, rows), lanes] for t in range(TAPS)]
        ask, gated, direct = features(0, lanes, shifted, skip[:, lanes])
        query[0, :, lanes] = ask
        base[0, :, lanes] = x[:, lanes] + direct
        move(row).start()
        send_products(0, row, gated, i == 0)
        return carry

    lax.fori_loop(0, SIDE, early_chunk, 0)
    pltpu.make_async_copy(product.at[0, ctx], got.at[0, ctx], prod_recv.at[0]).start()

    root[...] = jnp.broadcast_to(jnp.sqrt(mean), (rows, BLOCK)).T[:SIDE]
    smalls[3].start()
    smalls[2].wait_recv()
    kern_wide[:, 0, :] = kern[...].astype(jnp.float32).T[:HALF]
    kern_wide[:, 1, :] = kern_early[...].astype(jnp.float32).T[HALF:]
    kern_out[...] = kern_wide[...].astype(jnp.bfloat16)

    def at(dz, dy):
        return (z + dz) % SIDE * SIDE + (y + dy) % SIDE

    def send_kern(k, carry):
        to = at(k // SIDE * step_z, k % SIDE * step_y)
        remote(kern_out.at[to], kern_in.at[ctx], kern_send, kern_recv, ctx=to).start()
        return carry

    lax.fori_loop(1, HALF, send_kern, 0)
    pltpu.make_async_copy(kern_out.at[ctx], kern_in.at[ctx], kern_recv).start()

    for i in (0, 1, 3):
        smalls[i].wait_recv()
    for f in range(3):
        taps[1, f] = short_in[f].astype(jnp.float32)
    spread = jnp.broadcast_to(root_in[0:1, :], (rows, BLOCK)).T

    def wait_in(dst, sem):
        pltpu.make_async_copy(dst, dst, sem).wait()

    def late_chunk(i, carry):
        row = lane_row(i)
        lanes = pl.ds(pl.multiple_of(row * BLOCK, BLOCK), BLOCK)
        wait_in(moved_in.at[:, lanes], move_recv.at[row])
        shifted_in[...] = moved_in[:, lanes].astype(jnp.float32)
        shifted = [shifted_in[TOP - t : TOP - t + rows, :] for t in range(TAPS)]
        ask, gated, direct = features(1, lanes, shifted, skip_in[:, lanes])
        query[1, :, lanes] = ask
        base[1, :, lanes] = shifted[0] * spread + direct
        send_products(1, row, gated, i == 0)
        return carry

    lax.fori_loop(0, SIDE, late_chunk, 0)
    pltpu.make_async_copy(product.at[1, ctx], got.at[1, ctx], prod_recv.at[1]).start()

    wait_in(kern_in, kern_recv)
    kern_wide[...] = kern_in[...].astype(jnp.float32)
    spec = transform([kern_wide[:, h, :] for h in range(HALVES)], outer, forward, turn)
    for h in range(HALVES):
        filt[h] = spec[h * PAD : (h + 1) * PAD]

    for h in range(HALVES):
        wait_in(got.at[h], prod_recv.at[h])
        wide[...] = got[h].astype(jnp.float32).reshape(wide.shape)

        def group(g, carry):
            ids = [g * TOGETHER + j for j in range(TOGETHER)]
            slabs = [wide[pl.ds(c, HALF, stride=GROUP), :] for c in ids]
            spec = transform(slabs, outer, forward, turn)
            gain = filt[h]
            made = untransform(spec, TOGETHER, gain[:, :BLOCK], gain[:, BLOCK:], inverse, turn, final)
            for j, c in enumerate(ids):
                result[pl.ds(c, HALF, stride=GROUP), :] = made[:, j * BLOCK : (j + 1) * BLOCK]
            return carry

        lax.fori_loop(0, GROUP // TOGETHER, group, 0, unroll=True)
        ready[h] = result[...].reshape(HALF, GROUP, BLOCK).astype(jnp.bfloat16)

        def send_back(k, carry):
            to = at(k // SIDE * step_z, k % SIDE * step_y)
            remote(ready.at[h, to], conv.at[h, ctx], conv_send.at[h], conv_recv.at[h, z], ctx=to).start()
            return carry

        lax.fori_loop(1, HALF, send_back, 0)
        pltpu.make_async_copy(ready.at[h, ctx], conv.at[h, ctx], conv_recv.at[h, z]).start()

    def finish(h, row, lanes):
        blocks = pl.ds(row * SIDE, SIDE)
        wait_in(conv.at[h, blocks], conv_recv.at[h, row])
        got_conv = conv[h, blocks].astype(jnp.float32).reshape(BLOCK, BLOCK).T
        return base[h, :, lanes] + query[h, :, lanes] * got_conv

    def back_row(i):
        return (z + i * (SIDE - step_z)) % SIDE

    def finish_early(i, carry):
        row = back_row(i)
        lanes = pl.ds(pl.multiple_of(row * BLOCK, BLOCK), BLOCK)
        finished[:, lanes] = finish(0, row, lanes).astype(jnp.bfloat16)
        remote(finished.at[:, lanes], finished_in.at[:, lanes], hop_send, hop_recv.at[row], section=onward).start()
        return carry

    lax.fori_loop(0, SIDE, finish_early, 0)

    def take_early(i, carry):
        row = back_row(i)
        lanes = pl.ds(pl.multiple_of(row * BLOCK, BLOCK), BLOCK)
        wait_in(finished_in.at[:, lanes], hop_recv.at[row])
        out[:, lanes] = finished_in[:, lanes].astype(jnp.float32)
        return carry

    def finish_late(i, carry):
        row = back_row(i)
        lanes = pl.ds(pl.multiple_of(row * BLOCK, BLOCK), BLOCK)
        after = pl.ds(pl.multiple_of(part + row * BLOCK, BLOCK), BLOCK)
        out[:, after] = finish(1, row, lanes)
        return carry

    lax.fori_loop(0, SIDE, take_early, 0)
    lax.fori_loop(0, SIDE, finish_late, 0)

    sent = pl.ds(0, HALF - 1)
    for send in (swap, *edges, *smalls):
        send.wait_send()
    wait_in(moved, move_send)
    wait_in(kern_out.at[sent], kern_send)
    for h in range(HALVES):
        wait_in(product.at[h, sent], prod_send.at[h])
        wait_in(ready.at[h, sent], conv_send.at[h])
    wait_in(finished, hop_send)


def local(section_input, long_filter, short_filter, skip_gain):
    rows, chans = section_input.shape[1:]
    part = chans // HALVES
    args = (section_input[0], long_filter[0], short_filter[0], skip_gain, *tables())
    anywhere = pl.BlockSpec(memory_space=pl.ANY)
    f32, bf16 = jnp.float32, jnp.bfloat16
    dma = pltpu.SemaphoreType.DMA
    blocks = pltpu.VMEM((HALVES, HALF, GROUP, BLOCK), bf16)
    kernels = pltpu.VMEM((HALF, HALVES, BLOCK), bf16)
    scratch = [pltpu.VMEM(arg.shape, arg.dtype) for arg in args] + [
        pltpu.VMEM((HALO, chans), f32),
        pltpu.VMEM((HALO, chans), f32),
        pltpu.VMEM((HALO, BLOCK), f32),
        pltpu.VMEM((2, HALO, BLOCK), f32),
        pltpu.VMEM((rows, BLOCK), f32),
        pltpu.VMEM((rows, BLOCK), f32),
        pltpu.VMEM((SIDE, BLOCK), f32),
        pltpu.VMEM((SIDE, BLOCK), f32),
        pltpu.VMEM((3, TAPS, part), bf16),
        pltpu.VMEM((1, part), f32),
        pltpu.VMEM(args[1].shape, bf16),
        pltpu.VMEM((HALVES, 3, TAPS, part), f32),
        pltpu.VMEM((TOP + rows, part), f32),
        pltpu.VMEM((TOP + rows, part), bf16),
        pltpu.VMEM((TOP + rows, part), bf16),
        pltpu.VMEM((TOP + rows, BLOCK), f32),
        pltpu.VMEM((HALVES, rows, part), f32),
        pltpu.VMEM((HALVES, rows, part), f32),
        kernels, kernels, pltpu.VMEM((HALF, HALVES, BLOCK), f32),
        pltpu.VMEM((HALVES, PAD, 2 * BLOCK), f32),
        blocks, blocks,
        pltpu.VMEM((HALF * GROUP, BLOCK), f32),
        pltpu.VMEM((HALF * GROUP, BLOCK), f32),
        blocks, blocks,
        pltpu.VMEM((rows, part), bf16),
        pltpu.VMEM((rows, part), bf16),
        pltpu.SemaphoreType.REGULAR,
        dma((len(args),)),
        dma((3,)), dma((3,)),
        dma, dma,
        dma((4,)), dma((4,)),
        dma, dma((SIDE,)),
        dma, dma,
        dma((HALVES,)), dma((HALVES,)),
        dma((HALVES,)), dma((HALVES, SIDE)),
        dma, dma((SIDE,)),
    ]
    received = pl.pallas_call(
        tick,
        out_shape=jax.ShapeDtypeStruct((rows, chans), f32),
        in_specs=[anywhere] * len(args),
        out_specs=pl.BlockSpec(memory_space=pltpu.VMEM),
        scratch_shapes=scratch,
        compiler_params=pltpu.CompilerParams(collective_id=0, has_side_effects=True, vmem_limit_bytes=48 << 20),
        name="tick",
    )(*(pltpu.with_memory_space_constraint(arg, pltpu.HBM) for arg in args))
    return received[None]


def solution(mesh):
    in_specs = (
        P("section", "ctx", "tp"),
        P("section", "ctx", "tp"),
        P("section", None, None, "tp"),
        P("section", "tp"),
    )
    out_specs = P("section", "ctx", "tp")
    return jax.shard_map(local, mesh=mesh, in_specs=in_specs, out_specs=out_specs, check_vma=False)
```
